128 devices in a mesh: dp: 32 (over z, y, core), mp: 4 (over x).
Axes of the slice: x: 4, y: 4, z: 4, core: 2. Of those that a mesh axis runs over, the one named last changes fastest.
Arguments:
- features: bfloat16 [98304, 1024], P('dp'), may hold values from -6 to 6
- curvature: bfloat16 [98304, 4096], P('dp', 'mp'), may hold values from 0.099609375 to 2
- task_grad: float32 [1024, 4096], P('dp', 'mp'), may hold values from -6 to 6
Outputs:
- solution: float32 [1024, 4096], P('dp', 'mp')
- residual: float32 [1024, 4096], P('dp', 'mp')
The draws below stay inside these ranges and needn't reach their ends.
All inputs are finite; a program needn't handle non-finite values.
Results may differ from the reference program's by a relative error of at most 0.0095.
The reference program's roundings to bfloat16 on the way count: a program that leaves them out, or rounds other values in their place, can miss the bound.
Values may be sent and summed in bfloat16 or wider, within the bound.
A program may use at most 64 MiB of HBM per device.

```python
import math
import jax
import jax.numpy as jnp
from jax import lax

DIN = 1024
DOUT = 4096
TOK_DEV = 3072
ITERS = 2
TOKENS = 98304
N_DP = 32


def block_levels(key, extent, split, least, largest):
    factor_of = 1.0
    for axis_at, shards_of in split:
        heights = jax.random.uniform(jax.random.fold_in(jax.random.fold_in(key, 6), axis_at), (shards_of,), jnp.float32, least / len(split), largest / len(split))
        factor_of = factor_of * jnp.repeat(jnp.exp(heights), extent[axis_at] // shards_of).reshape((-1,) + (1,) * (len(extent) - 1 - axis_at))
    return factor_of


def bell_draw(rng, extent, deviation, most, pieces=(), dtype=jnp.bfloat16):
    loudness = block_levels(rng, extent, pieces, -0.22, 0.18) if pieces else 1.0
    result = jax.random.normal(rng, extent, jnp.float32) * deviation * loudness
    return jnp.minimum(jnp.maximum(result, -most), most).astype(dtype)


def setup_inputs(seed: int = 0) -> dict:
    key_list = jax.random.split(jax.random.key(seed), 4)
    return {
        "features": bell_draw(key_list[0], (TOKENS, DIN), 1.0, 6.0, ((0, 32),)),
        "curvature": jnp.clip(jnp.exp(math.log(2.0) - 2.9996462 * jax.random.uniform(key_list[1], (TOKENS, DOUT), jnp.float32) ** block_levels(key_list[1], (TOKENS, DOUT), ((0, 32), (1, 4)), -0.2, 0.2)), 0.099609375, 2.0).astype(jnp.bfloat16),
        "task_grad": bell_draw(key_list[2], (DIN, DOUT), 1.0, 6.0, ((0, 32), (1, 4)), jnp.float32),
    }


damp_coef = 0.5


def apply_operator(features, curvature, direction):
    dir_bf = direction.astype(jnp.bfloat16)
    feat_blocks = features.reshape(N_DP, TOK_DEV, DIN)
    curv_blocks = curvature.reshape(N_DP, TOK_DEV, DOUT)

    def add_block(accum, blocks):
        feat_rows, curv_rows = blocks
        projected = jnp.dot(feat_rows, dir_bf, preferred_element_type=jnp.float32)
        weighted = (curv_rows.astype(jnp.float32) * projected).astype(jnp.bfloat16)
        return accum + jnp.dot(feat_rows.T, weighted, preferred_element_type=jnp.float32), None

    accum, unused = lax.scan(add_block, jnp.zeros((DIN, DOUT), jnp.float32), (feat_blocks, curv_blocks))
    return accum / TOKENS + damp_coef * direction


def reference(features, curvature, task_grad):
    solution = jnp.zeros_like(task_grad)
    residual = task_grad
    direction = task_grad
    norm_now = jnp.sum(residual * residual)
    for turn in range(ITERS):
        curved = apply_operator(features, curvature, direction)
        step_len = norm_now / jnp.sum(direction * curved)
        solution = solution + step_len * direction
        residual = residual - step_len * curved
        if turn + 1 < ITERS:
            norm_next = jnp.sum(residual * residual)
            direction = residual + (norm_next / norm_now) * direction
            norm_now = norm_next
    return solution, residual
```

```python
import functools

import jax
import jax.numpy as jnp
from jax import lax
from jax.experimental import pallas as pl
from jax.experimental.pallas import tpu as pltpu
from jax.sharding import PartitionSpec as P

RING = 4
GROUP = 32
N_MP = 4
TOK = 3072
DIN = 1024
COLS = 1024
NB = 256
BLOCKS = COLS // NB
ROWS = DIN // GROUP
TOKENS = 98304.0
DAMP = 0.5
MC = 1536
MESH = pl.DeviceIdType.MESH
BF, F32 = jnp.bfloat16, jnp.float32


def kernel(
    f_h, c_h, g_h, sol_h, res_h,
    f, ft, cv, g, d, w, sol, vb, g_own, g_par, v, wt,
    acc, accb, d0, d0b, s, sb, rin, rinb, xy, xyb, t, r2in,
    row, tab, row2, tab2,
    ss, rs, ts, tr, ts2, tr2, ld,
):
    me = lax.axis_index("dp")
    mx = lax.axis_index("mp")
    c = lax.rem(me, 2)
    chip = me // 2
    z = chip // RING
    y = lax.rem(chip, RING)
    pa = (1 - c) * y + c * z
    pb = (1 - c) * z + c * y

    def a_at(k):
        q = lax.rem(pa + k, RING)
        return ((1 - c) * (z * RING + q) + c * (q * RING + y)) * 2 + c

    def b_at(k):
        q = lax.rem(pb + k, RING)
        return ((1 - c) * (q * RING + y) + c * (z * RING + q)) * 2 + c

    partner = me + 1 - 2 * c
    a_up, a_dn, a_op = a_at(1), a_at(3), a_at(2)
    b_up, b_dn, b_op = b_at(1), b_at(3), b_at(2)
    qa_up, qa_dn, qa_op = lax.rem(pa + 1, RING), lax.rem(pa + 3, RING), lax.rem(pa + 2, RING)
    qb_up, qb_dn, qb_op = lax.rem(pb + 1, RING), lax.rem(pb + 3, RING), lax.rem(pb + 2, RING)

    loads = [
        pltpu.make_async_copy(g_h.at[:, pl.ds(j * NB, NB)], g.at[j], ld.at[j])
        for j in range(BLOCKS)
    ]
    parts = 4
    f_loads = [
        pltpu.make_async_copy(
            f_h.at[pl.ds(k * (TOK // parts), TOK // parts)],
            f.at[pl.ds(k * (TOK // parts), TOK // parts)],
            ld.at[BLOCKS + k],
        )
        for k in range(parts)
    ]
    c_load = pltpu.make_async_copy(c_h, cv, ld.at[BLOCKS + parts])
    for x in (*loads, *f_loads, c_load):
        x.start()

    barrier = pltpu.get_barrier_semaphore()

    @pl.loop(1, GROUP)
    def _(k):
        pl.semaphore_signal(
            barrier, inc=1, device_id={"dp": lax.rem(me + k, GROUP)}, device_id_type=MESH
        )

    for k in range(1, N_MP):
        pl.semaphore_signal(
            barrier, inc=1, device_id={"mp": lax.rem(mx + k, N_MP)}, device_id_type=MESH
        )

    def copy(j, i, src, dst, dev):
        return pltpu.make_async_remote_copy(
            src_ref=src, dst_ref=dst, send_sem=ss.at[j, i], recv_sem=rs.at[j, i],
            device_id={"dp": dev}, device_id_type=MESH,
        )

    def send(j, i, src, dst, dev):
        copy(j, i, src, dst, dev).start()

    def got(j, i, dst):
        copy(j, i, dst, dst, partner).wait_recv()

    def sent(j, i, src):
        copy(j, i, src, src, partner).wait_send()

    def strip(buf, j, q):
        return buf.at[j, pl.ds(q * RING, RING)]

    def ag1(j):
        dst = g_own.at[j, pb * RING + pa]
        send(j, 0, vb.at[j], dst, a_up)
        send(j, 1, vb.at[j], dst, a_dn)
        send(j, 2, vb.at[j], dst, a_op)
        g_own[j, pb * RING + pa] = vb[j]

    def ag2(j):
        got(j, 0, g_own.at[j, pb * RING + qa_dn])
        got(j, 1, g_own.at[j, pb * RING + qa_up])
        got(j, 2, g_own.at[j, pb * RING + qa_op])
        mine = strip(g_own, j, pb)
        send(j, 3, mine, mine, b_up)
        send(j, 4, mine, mine, b_dn)
        send(j, 7, mine, strip(g_par, j, pb), partner)

    def ag3(j):
        below, above = strip(g_own, j, qb_dn), strip(g_own, j, qb_up)
        got(j, 3, below)
        half = g_own.at[j, pl.ds(qb_dn * RING, 2)]
        send(j, 5, half, half, b_up)
        send(j, 8, below, strip(g_par, j, qb_dn), partner)
        got(j, 4, above)
        half = g_own.at[j, pl.ds(qb_up * RING + 2, 2)]
        send(j, 6, half, half, b_dn)
        send(j, 9, above, strip(g_par, j, qb_up), partner)

    def ag4(j):
        got(j, 5, g_own.at[j, pl.ds(qb_op * RING, 2)])
        got(j, 6, g_own.at[j, pl.ds(qb_op * RING + 2, 2)])
        send(j, 10, strip(g_own, j, qb_op), strip(g_par, j, qb_op), partner)

    def ag5(j):
        got(j, 7, strip(g_par, j, pa))
        got(j, 8, strip(g_par, j, qa_dn))
        got(j, 9, strip(g_par, j, qa_up))
        got(j, 10, strip(g_par, j, qa_op))
        for zz in range(RING):
            for yy in range(RING):
                zy, yz = zz * RING + yy, yy * RING + zz
                v[j, zz, yy, c] = g_own[j, (1 - c) * zy + c * yz]
                v[j, zz, yy, 1 - c] = g_par[j, (1 - c) * yz + c * zy]

    def p1(j, m):
        r = pl.ds(m * MC, MC)
        cols = pl.ds(pl.multiple_of(j * NB, NB), NB)
        p = jnp.dot(f[r, :], v[j].reshape(DIN, NB), preferred_element_type=F32)
        wt[r, :] = (cv[r, cols].astype(F32) * p).astype(BF)

    def p2(j, h, low):
        out = jnp.dot(ft[pl.ds(h * (DIN // 2), DIN // 2), :], wt[...], preferred_element_type=F32)
        out = out.reshape(2, RING, 2, ROWS, NB)
        acc[j, pl.ds(2 * h, 2)] = out
        if low:
            accb[j, pl.ds(2 * h, 2)] = out.astype(BF)
            send(j, 11 + h, accb.at[j, pl.ds(2 * h, 2), :, 1 - c], d0b.at[j, pl.ds(2 * h, 2)], partner)
        else:
            send(j, 11 + h, acc.at[j, pl.ds(2 * h, 2), :, 1 - c], d0.at[j, pl.ds(2 * h, 2)], partner)

    def r1(j, low):
        src, inn, sm = (d0b, rinb, sb) if low else (d0, rin, s)
        for h in range(2):
            got(j, 11 + h, src.at[j, pl.ds(2 * h, 2)])
            for zz in (2 * h, 2 * h + 1):
                for yy in range(RING):
                    zy, yz = zz * RING + yy, yy * RING + zz
                    both = acc[j, zz, yy, c] + src[j, zz, yy].astype(F32)
                    s[j, (1 - c) * yz + c * zy] = both
                    if low:
                        sb[j, (1 - c) * yz + c * zy] = both.astype(BF)
        send(j, 13, sm.at[j, pl.ds(qa_op * RING, 2)], inn.at[j, 0], a_up)
        send(j, 14, sm.at[j, pl.ds(qa_op * RING + 2, 2)], inn.at[j, 1], a_dn)
        send(j, 15, sm.at[j, pl.ds(qa_up * RING + 2, 2)], inn.at[j, 2], a_up)
        send(j, 16, sm.at[j, pl.ds(qa_dn * RING, 2)], inn.at[j, 3], a_dn)

    def r2(j, low):
        inn, out = (rinb, xyb) if low else (rin, xy)
        got(j, 13, inn.at[j, 0])
        out[j, 0] = (inn[j, 0].astype(F32) + s[j, pl.ds(qa_up * RING, 2)]).astype(out.dtype)
        send(j, 17, out.at[j, 0], inn.at[j, 4], a_up)
        got(j, 14, inn.at[j, 1])
        out[j, 1] = (inn[j, 1].astype(F32) + s[j, pl.ds(qa_dn * RING + 2, 2)]).astype(out.dtype)
        send(j, 18, out.at[j, 1], inn.at[j, 5], a_dn)

    def r3(j, low):
        inn = rinb if low else rin
        for i in (15, 16, 17, 18):
            got(j, i, inn.at[j, i - 13])
        mine = s[j, pl.ds(pa * RING, RING)]
        t[j, pl.ds(0, 2)] = mine[:2] + (inn[j, 4].astype(F32) + inn[j, 3].astype(F32))
        t[j, pl.ds(2, 2)] = mine[2:] + (inn[j, 2].astype(F32) + inn[j, 5].astype(F32))
        send(j, 19, t.at[j, qb_up], r2in.at[j, 0], b_up)
        send(j, 20, t.at[j, qb_dn], r2in.at[j, 1], b_dn)
        send(j, 21, t.at[j, qb_op], r2in.at[j, 2], b_op)

    def r4(j):
        for i in (19, 20, 21):
            got(j, i, r2in.at[j, i - 19])
        total = (t[j, pb] + r2in[j, 2]) + (r2in[j, 0] + r2in[j, 1])
        w[j] = total / TOKENS + DAMP * d[j]

    def drain_gather():
        @pl.loop(0, BLOCKS)
        def _(j):
            for i in range(3):
                sent(j, i, vb.at[j])
            for i in (3, 4, 7, 8, 9, 10):
                sent(j, i, strip(g_own, j, 0))
            for i in (5, 6):
                sent(j, i, g_own.at[j, pl.ds(0, 2)])

    def drain(low):
        @pl.loop(0, BLOCKS)
        def _(j):
            for i in (11, 12):
                sent(j, i, (d0b if low else d0).at[j, pl.ds(0, 2)])
            for i in range(13, 19):
                sent(j, i, (rinb if low else rin).at[j, 0])
            for i in range(19, 22):
                sent(j, i, t.at[j, 0])

    def operator(first):
        low = not first

        def transpose(k0, k1):
            if first:

                @pl.loop(k0, k1)
                def _(k):
                    r = pl.ds(pl.multiple_of(k * 256, 256), 256)
                    ft[:, r] = f[r, :].T

        for j in range(BLOCKS):
            vb[j] = d[j].astype(BF)
        if first:
            pl.semaphore_wait(barrier, GROUP - 1 + N_MP - 1)

        @pl.loop(0, BLOCKS)
        def _(j):
            ag1(j)

        if first:
            f_loads[0].wait()
            f_loads[1].wait()
        transpose(0, 4)
        ag2(0)
        ag2(1)
        if first:
            f_loads[2].wait()
        transpose(4, 8)
        ag3(0)
        if first:
            f_loads[3].wait()
        transpose(8, 12)
        ag4(0)
        if first:
            c_load.wait()
        ag5(0)

        @pl.loop(0, BLOCKS)
        def _(j):
            p1(j, 0)

            @pl.when(j < BLOCKS - 1)
            def _():
                ag3(j + 1)

            p1(j, 1)

            @pl.when(j < BLOCKS - 1)
            def _():
                ag4(j + 1)

            @pl.when(j >= 1)
            def _():
                r1(j - 1, low)

            @pl.when(j >= 2)
            def _():
                r3(j - 2, low)

            p2(j, 0, low)

            @pl.when(j < BLOCKS - 2)
            def _():
                ag2(j + 2)

            p2(j, 1, low)

            @pl.when(j >= 1)
            def _():
                r2(j - 1, low)

            @pl.when(j >= 2)
            def _():
                r4(j - 2)

            @pl.when(j < BLOCKS - 1)
            def _():
                ag5(j + 1)

        last = BLOCKS - 1
        r1(last, low)
        r3(last - 1, low)
        r2(last, low)
        r4(last - 1)
        r3(last, low)
        r4(last)

    def total(x):
        return jnp.sum(jnp.sum(jnp.sum(x, axis=0), axis=0, keepdims=True), axis=1, keepdims=True)

    def put(buf, i, values):
        buf[i] = jnp.zeros((8, 128), F32)
        for k, x in enumerate(values):
            buf[i, pl.ds(k, 1), :] = jnp.broadcast_to(x, (1, 128))

    def exchange(turn, values, middle, meanwhile):
        put(row, turn, values)

        @pl.loop(1, GROUP)
        def _(k):
            pltpu.make_async_remote_copy(
                src_ref=row.at[turn], dst_ref=tab.at[turn, me],
                send_sem=ts.at[turn, k], recv_sem=tr.at[turn, me],
                device_id={"dp": lax.rem(me + k, GROUP)}, device_id_type=MESH,
            ).start()

        tab[turn, me] = row[turn]
        meanwhile()

        @pl.loop(1, GROUP)
        def _(k):
            q = lax.rem(me + k, GROUP)
            pltpu.make_async_remote_copy(
                src_ref=row.at[turn], dst_ref=tab.at[turn, q],
                send_sem=ts.at[turn, k], recv_sem=tr.at[turn, q],
                device_id={"dp": q}, device_id_type=MESH,
            ).wait()

        put(row2, turn, middle(tab[turn]))
        out = [
            pltpu.make_async_remote_copy(
                src_ref=row2.at[turn], dst_ref=tab2.at[turn, mx],
                send_sem=ts2.at[turn, k], recv_sem=tr2.at[turn, k],
                device_id={"mp": lax.rem(mx + k, N_MP)}, device_id_type=MESH,
            )
            for k in range(1, N_MP)
        ]
        for x in out:
            x.start()
        tab2[turn, mx] = row2[turn]
        for k in range(1, N_MP):
            q = lax.rem(mx + N_MP - k, N_MP)
            pltpu.make_async_remote_copy(
                src_ref=row2.at[turn], dst_ref=tab2.at[turn, q],
                send_sem=ts2.at[turn, k], recv_sem=tr2.at[turn, k],
                device_id={"mp": q}, device_id_type=MESH,
            ).wait()
        return tab2[turn]

    def column(tb, k):
        return tb[:, k : k + 1, :]

    def moved(tb, x):
        ww, uu, uw, at = (column(tb, k) for k in (2, 3, 4, 5))
        gap = at - x
        return jnp.sum(uu + gap * (2.0 * uw + gap * ww), axis=0), jnp.sum(uw + gap * ww, axis=0)

    def ratio(p, q):
        return jnp.where(q > 0, p / jnp.where(q > 0, q, 1.0), 0.0)

    def centre(tb):
        gg, gw, ww = (jnp.sum(column(tb, k), axis=0) for k in range(3))
        x = ratio(gw, ww)
        uu, uw = moved(tb, x)
        return gg, gw, ww, uu, uw, x

    for x in loads:
        x.wait()
    d[...] = g[...]
    operator(True)
    gv, wv = g[...], w[...]
    gg, gw, ww = total(gv * gv), total(gv * wv), total(wv * wv)
    x = ratio(gw, ww)
    u = gv - x * wv
    drain_gather()
    tb = exchange(0, (gg, gw, ww, total(u * u), total(u * wv), x), centre, lambda: drain(False))
    norm = jnp.sum(column(tb, 0), axis=0)
    step = norm / jnp.sum(column(tb, 1), axis=0)
    norm_next, _ = moved(tb, step)
    beta = norm_next / norm
    step = step[:, :1]
    sol[...] = step * gv
    res = gv - step * wv
    g[...] = res
    d[...] = res + beta[:, :1] * gv
    operator(False)
    dv, wv = d[...], w[...]
    tb = exchange(1, (total(dv * wv),), lambda tb: (jnp.sum(column(tb, 0), axis=0),), lambda: drain(True))
    step = (norm_next / jnp.sum(column(tb, 0), axis=0))[:, :1]
    sol[...] = sol[...] + step * dv
    g[...] = g[...] - step * wv
    outs = [
        pltpu.make_async_copy(b.at[j], o.at[:, pl.ds(j * NB, NB)], ld.at[k * BLOCKS + j])
        for k, (b, o) in enumerate(((sol, sol_h), (g, res_h)))
        for j in range(BLOCKS)
    ]
    for x in outs:
        x.start()
    drain_gather()
    for x in outs:
        x.wait()


def shards(features, curvature, task_grad):
    any_spec = pl.BlockSpec(memory_space=pl.ANY)
    out = jax.ShapeDtypeStruct(task_grad.shape, F32)
    small = (BLOCKS, ROWS, NB)
    return pl.pallas_call(
        kernel,
        out_shape=(out, out),
        in_specs=[any_spec] * 3,
        out_specs=(any_spec, any_spec),
        scratch_shapes=[
            pltpu.VMEM((TOK, DIN), BF),
            pltpu.VMEM((DIN, TOK), BF),
            pltpu.VMEM((TOK, COLS), BF),
            pltpu.VMEM(small, F32),
            pltpu.VMEM(small, F32),
            pltpu.VMEM(small, F32),
            pltpu.VMEM(small, F32),
            pltpu.VMEM(small, BF),
            pltpu.VMEM((BLOCKS, 16, ROWS, NB), BF),
            pltpu.VMEM((BLOCKS, 16, ROWS, NB), BF),
            pltpu.VMEM((BLOCKS, RING, RING, 2, ROWS, NB), BF),
            pltpu.VMEM((TOK, NB), BF),
            pltpu.VMEM((BLOCKS, RING, RING, 2, ROWS, NB), F32),
            pltpu.VMEM((BLOCKS, RING, RING, 2, ROWS, NB), BF),
            pltpu.VMEM((BLOCKS, RING, RING, ROWS, NB), F32),
            pltpu.VMEM((BLOCKS, RING, RING, ROWS, NB), BF),
            pltpu.VMEM((BLOCKS, 16, ROWS, NB), F32),
            pltpu.VMEM((BLOCKS, 16, ROWS, NB), BF),
            pltpu.VMEM((BLOCKS, 6, 2, ROWS, NB), F32),
            pltpu.VMEM((BLOCKS, 6, 2, ROWS, NB), BF),
            pltpu.VMEM((BLOCKS, 2, 2, ROWS, NB), F32),
            pltpu.VMEM((BLOCKS, 2, 2, ROWS, NB), BF),
            pltpu.VMEM((BLOCKS, RING, ROWS, NB), F32),
            pltpu.VMEM((BLOCKS, 3, ROWS, NB), F32),
            pltpu.VMEM((2, 8, 128), F32),
            pltpu.VMEM((2, GROUP, 8, 128), F32),
            pltpu.VMEM((2, 8, 128), F32),
            pltpu.VMEM((2, N_MP, 8, 128), F32),
            pltpu.SemaphoreType.DMA((BLOCKS, 22)),
            pltpu.SemaphoreType.DMA((BLOCKS, 22)),
            pltpu.SemaphoreType.DMA((2, GROUP)),
            pltpu.SemaphoreType.DMA((2, GROUP)),
            pltpu.SemaphoreType.DMA((2, N_MP)),
            pltpu.SemaphoreType.DMA((2, N_MP)),
            pltpu.SemaphoreType.DMA((2 * BLOCKS + 1,)),
        ],
        compiler_params=pltpu.CompilerParams(
            collective_id=0, has_side_effects=True, vmem_limit_bytes=62 * 2**20
        ),
    )(features, curvature, task_grad)


def solution(mesh):
    placed = (P("dp", None), P("dp", "mp"), P("dp", "mp"))
    return jax.shard_map(
        shards,
        mesh=mesh,
        in_specs=placed,
        out_specs=(P("dp", "mp"), P("dp", "mp")),
        check_vma=False,
    )
```

```python
import functools

import jax
import jax.numpy as jnp
from jax import lax
from jax.experimental import pallas as pl
from jax.experimental.pallas import tpu as pltpu
from jax.sharding import PartitionSpec as P

RING = 4
GROUP = 32
N_MP = 4
TOK = 3072
DIN = 1024
COLS = 1024
NB = 256
BLOCKS = COLS // NB
ROWS = DIN // GROUP
TOKENS = 98304.0
DAMP = 0.5
MC = 1536
MESH = pl.DeviceIdType.MESH
BF, F32 = jnp.bfloat16, jnp.float32


def kernel(
    f_h, c_h, g_h, sol_h, res_h,
    f, ft, cv, g, d, w, sol, vb, g_own, g_par, v, wt,
    acc, accb, d0, d0b, s, sb, rin, rinb, t, r2in,
    row, tab, row2, tab2,
    ss, rs, ts, tr, ts2, tr2, ld,
):
    me = lax.axis_index("dp")
    mx = lax.axis_index("mp")
    c = lax.rem(me, 2)
    chip = me // 2
    z = chip // RING
    y = lax.rem(chip, RING)
    pa = (1 - c) * y + c * z
    pb = (1 - c) * z + c * y

    def a_at(k):
        q = lax.rem(pa + k, RING)
        return ((1 - c) * (z * RING + q) + c * (q * RING + y)) * 2 + c

    def b_at(k):
        q = lax.rem(pb + k, RING)
        return ((1 - c) * (q * RING + y) + c * (z * RING + q)) * 2 + c

    partner = me + 1 - 2 * c
    a_up, a_dn, a_op = a_at(1), a_at(3), a_at(2)
    b_up, b_dn, b_op = b_at(1), b_at(3), b_at(2)
    qa_up, qa_dn, qa_op = lax.rem(pa + 1, RING), lax.rem(pa + 3, RING), lax.rem(pa + 2, RING)
    qb_up, qb_dn, qb_op = lax.rem(pb + 1, RING), lax.rem(pb + 3, RING), lax.rem(pb + 2, RING)

    loads = [
        pltpu.make_async_copy(g_h.at[:, pl.ds(j * NB, NB)], g.at[j], ld.at[j])
        for j in range(BLOCKS)
    ]
    parts = 4
    f_loads = [
        pltpu.make_async_copy(
            f_h.at[pl.ds(k * (TOK // parts), TOK // parts)],
            f.at[pl.ds(k * (TOK // parts), TOK // parts)],
            ld.at[BLOCKS + k],
        )
        for k in range(parts)
    ]
    c_load = pltpu.make_async_copy(c_h, cv, ld.at[BLOCKS + parts])
    for x in (*loads, *f_loads, c_load):
        x.start()

    barrier = pltpu.get_barrier_semaphore()

    for q in (a_up, a_dn, a_op, b_up, b_dn, b_op, partner):
        pl.semaphore_signal(barrier, inc=1, device_id={"dp": q}, device_id_type=MESH)

    for k in range(1, N_MP):
        pl.semaphore_signal(
            barrier, inc=1, device_id={"mp": lax.rem(mx + k, N_MP)}, device_id_type=MESH
        )

    def copy(j, i, src, dst, dev):
        return pltpu.make_async_remote_copy(
            src_ref=src, dst_ref=dst, send_sem=ss.at[j, i], recv_sem=rs.at[j, i],
            device_id={"dp": dev}, device_id_type=MESH,
        )

    def send(j, i, src, dst, dev):
        copy(j, i, src, dst, dev).start()

    def got(j, i, dst):
        copy(j, i, dst, dst, partner).wait_recv()

    def sent(j, i, src):
        copy(j, i, src, src, partner).wait_send()

    def strip(buf, j, q):
        return buf.at[j, pl.ds(q * RING, RING)]

    def ag1(j):
        dst = g_own.at[j, pb * RING + pa]
        send(j, 0, vb.at[j], dst, a_up)
        send(j, 1, vb.at[j], dst, a_dn)
        send(j, 2, vb.at[j], dst, a_op)
        g_own[j, pb * RING + pa] = vb[j]

    def ag2(j):
        got(j, 0, g_own.at[j, pb * RING + qa_dn])
        got(j, 1, g_own.at[j, pb * RING + qa_up])
        got(j, 2, g_own.at[j, pb * RING + qa_op])
        mine = strip(g_own, j, pb)
        send(j, 3, mine, mine, b_up)
        send(j, 4, mine, mine, b_dn)
        send(j, 5, mine, mine, b_op)
        send(j, 6, mine, strip(g_par, j, pb), partner)

    def ag3(j):
        for i, q in ((3, qb_dn), (4, qb_up), (5, qb_op)):
            got(j, i, strip(g_own, j, q))
            send(j, i + 4, strip(g_own, j, q), strip(g_par, j, q), partner)

    def ag5(j):
        got(j, 6, strip(g_par, j, pa))
        got(j, 7, strip(g_par, j, qa_dn))
        got(j, 8, strip(g_par, j, qa_up))
        got(j, 9, strip(g_par, j, qa_op))
        for zz in range(RING):
            for yy in range(RING):
                zy, yz = zz * RING + yy, yy * RING + zz
                v[j, zz, yy, c] = g_own[j, (1 - c) * zy + c * yz]
                v[j, zz, yy, 1 - c] = g_par[j, (1 - c) * yz + c * zy]

    def alone(j):
        return pl.loop(0, (j + BLOCKS) // BLOCKS)

    def p1(j, m):
        r = pl.ds(m * MC, MC)
        cols = pl.ds(pl.multiple_of(j * NB, NB), NB)

        @alone(j)
        def _(_):
            p = jnp.dot(f[r, :], v[j].reshape(DIN, NB), preferred_element_type=F32)
            wt[r, :] = (cv[r, cols].astype(F32) * p).astype(BF)

    def p2(j, h, low):
        r = pl.ds(h * (DIN // 2), DIN // 2)
        zs = pl.ds(2 * h, 2)

        @alone(j)
        def _(_):
            out = jnp.dot(ft[r, :], wt[...], preferred_element_type=F32)
            out = out.reshape(2, RING, 2, ROWS, NB)
            acc[j, zs] = out
            if low:
                accb[j, zs] = out.astype(BF)

        src, dst = (accb, d0b) if low else (acc, d0)
        send(j, 10 + h, src.at[j, zs, :, 1 - c], dst.at[j, zs], partner)

    def r1(j, low):
        src, inn, sm = (d0b, rinb, sb) if low else (d0, rin, s)
        for h in range(2):
            got(j, 10 + h, src.at[j, pl.ds(2 * h, 2)])
            for zz in (2 * h, 2 * h + 1):
                for yy in range(RING):
                    zy, yz = zz * RING + yy, yy * RING + zz
                    both = acc[j, zz, yy, c] + src[j, zz, yy].astype(F32)
                    s[j, (1 - c) * yz + c * zy] = both
                    if low:
                        sb[j, (1 - c) * yz + c * zy] = both.astype(BF)
        send(j, 12, strip(sm, j, qa_up), inn.at[j, 0], a_up)
        send(j, 13, strip(sm, j, qa_dn), inn.at[j, 1], a_dn)
        send(j, 14, strip(sm, j, qa_op), inn.at[j, 2], a_op)

    def r3(j, low):
        inn = rinb if low else rin
        for i in range(3):
            got(j, 12 + i, inn.at[j, i])
        mine = s[j, pl.ds(pa * RING, RING)]
        t[j] = (mine + inn[j, 2].astype(F32)) + (inn[j, 0].astype(F32) + inn[j, 1].astype(F32))
        send(j, 15, t.at[j, qb_up], r2in.at[j, 0], b_up)
        send(j, 16, t.at[j, qb_dn], r2in.at[j, 1], b_dn)
        send(j, 17, t.at[j, qb_op], r2in.at[j, 2], b_op)

    def r4(j):
        for i in range(3):
            got(j, 15 + i, r2in.at[j, i])
        total = (t[j, pb] + r2in[j, 2]) + (r2in[j, 0] + r2in[j, 1])
        w[j] = total / TOKENS + DAMP * d[j]

    def drain_gather():
        @pl.loop(0, BLOCKS)
        def _(j):
            for i in range(3):
                sent(j, i, vb.at[j])
            for i in range(3, 10):
                sent(j, i, strip(g_own, j, 0))

    def drain(low):
        @pl.loop(0, BLOCKS)
        def _(j):
            for i in (10, 11):
                sent(j, i, (d0b if low else d0).at[j, pl.ds(0, 2)])
            for i in (12, 13, 14):
                sent(j, i, (rinb if low else rin).at[j, 0])
            for i in (15, 16, 17):
                sent(j, i, t.at[j, 0])

    def operator(first):
        low = not first

        def transpose(k0, k1):
            if first:

                @pl.loop(k0, k1)
                def _(k):
                    r = pl.ds(pl.multiple_of(k * 256, 256), 256)
                    ft[:, r] = f[r, :].T

        for j in range(BLOCKS):
            vb[j] = d[j].astype(BF)
        if first:
            pl.semaphore_wait(barrier, 7 + N_MP - 1)

        ag1(0)
        ag1(1)
        if first:
            f_loads[0].wait()
            f_loads[1].wait()
        transpose(0, 6)
        ag2(0)
        ag1(2)
        ag1(3)
        ag2(1)
        if first:
            f_loads[2].wait()
            f_loads[3].wait()
        transpose(6, 12)
        ag3(0)
        if first:
            c_load.wait()
        ag5(0)

        @pl.loop(0, BLOCKS)
        def _(j):
            p1(j, 0)

            @pl.when(j < BLOCKS - 1)
            def _():
                ag3(j + 1)

            @pl.when(j >= 1)
            def _():
                r1(j - 1, low)

            p1(j, 1)

            @pl.when(j < BLOCKS - 2)
            def _():
                ag2(j + 2)

            @pl.when(j >= 2)
            def _():
                r3(j - 2, low)

            p2(j, 0, low)

            @pl.when(j < BLOCKS - 1)
            def _():
                ag5(j + 1)

            p2(j, 1, low)

            @pl.when(j >= 2)
            def _():
                r4(j - 2)

        last = BLOCKS - 1
        r1(last, low)
        r3(last - 1, low)
        r4(last - 1)
        r3(last, low)
        r4(last)

    def total(x):
        return jnp.sum(jnp.sum(jnp.sum(x, axis=0), axis=0, keepdims=True), axis=1, keepdims=True)

    def put(buf, i, values):
        buf[i] = jnp.zeros((8, 128), F32)
        for k, x in enumerate(values):
            buf[i, pl.ds(k, 1), :] = jnp.broadcast_to(x, (1, 128))

    def exchange(turn, values, middle, meanwhile):
        put(row, turn, values)

        @pl.loop(1, GROUP)
        def _(k):
            pltpu.make_async_remote_copy(
                src_ref=row.at[turn], dst_ref=tab.at[turn, me],
                send_sem=ts.at[turn, k], recv_sem=tr.at[turn, me],
                device_id={"dp": lax.rem(me + k, GROUP)}, device_id_type=MESH,
            ).start()

        tab[turn, me] = row[turn]
        meanwhile()

        @pl.loop(1, GROUP)
        def _(k):
            q = lax.rem(me + k, GROUP)
            pltpu.make_async_remote_copy(
                src_ref=row.at[turn], dst_ref=tab.at[turn, q],
                send_sem=ts.at[turn, k], recv_sem=tr.at[turn, q],
                device_id={"dp": q}, device_id_type=MESH,
            ).wait()

        put(row2, turn, middle(tab[turn]))
        out = [
            pltpu.make_async_remote_copy(
                src_ref=row2.at[turn], dst_ref=tab2.at[turn, mx],
                send_sem=ts2.at[turn, k], recv_sem=tr2.at[turn, k],
                device_id={"mp": lax.rem(mx + k, N_MP)}, device_id_type=MESH,
            )
            for k in range(1, N_MP)
        ]
        for x in out:
            x.start()
        tab2[turn, mx] = row2[turn]
        for k in range(1, N_MP):
            q = lax.rem(mx + N_MP - k, N_MP)
            pltpu.make_async_remote_copy(
                src_ref=row2.at[turn], dst_ref=tab2.at[turn, q],
                send_sem=ts2.at[turn, k], recv_sem=tr2.at[turn, k],
                device_id={"mp": q}, device_id_type=MESH,
            ).wait()
        return tab2[turn]

    def column(tb, k):
        return tb[:, k : k + 1, :]

    def moved(tb, x):
        ww, uu, uw, at = (column(tb, k) for k in (2, 3, 4, 5))
        gap = at - x
        return jnp.sum(uu + gap * (2.0 * uw + gap * ww), axis=0), jnp.sum(uw + gap * ww, axis=0)

    def ratio(p, q):
        return jnp.where(q > 0, p / jnp.where(q > 0, q, 1.0), 0.0)

    def centre(tb):
        gg, gw, ww = (jnp.sum(column(tb, k), axis=0) for k in range(3))
        x = ratio(gw, ww)
        uu, uw = moved(tb, x)
        return gg, gw, ww, uu, uw, x

    for x in loads:
        x.wait()
    d[...] = g[...]
    operator(True)
    gv, wv = g[...], w[...]
    gg, gw, ww = total(gv * gv), total(gv * wv), total(wv * wv)
    x = ratio(gw, ww)
    u = gv - x * wv
    drain_gather()
    tb = exchange(0, (gg, gw, ww, total(u * u), total(u * wv), x), centre, lambda: drain(False))
    norm = jnp.sum(column(tb, 0), axis=0)
    step = norm / jnp.sum(column(tb, 1), axis=0)
    norm_next, _ = moved(tb, step)
    beta = norm_next / norm
    step = step[:, :1]
    sol[...] = step * gv
    res = gv - step * wv
    g[...] = res
    d[...] = res + beta[:, :1] * gv
    operator(False)
    dv, wv = d[...], w[...]
    tb = exchange(1, (total(dv * wv),), lambda tb: (jnp.sum(column(tb, 0), axis=0),), lambda: drain(True))
    step = (norm_next / jnp.sum(column(tb, 0), axis=0))[:, :1]
    sol[...] = sol[...] + step * dv
    g[...] = g[...] - step * wv
    outs = [
        pltpu.make_async_copy(b.at[j], o.at[:, pl.ds(j * NB, NB)], ld.at[k * BLOCKS + j])
        for k, (b, o) in enumerate(((sol, sol_h), (g, res_h)))
        for j in range(BLOCKS)
    ]
    for x in outs:
        x.start()
    drain_gather()
    for x in outs:
        x.wait()


def shards(features, curvature, task_grad):
    any_spec = pl.BlockSpec(memory_space=pl.ANY)
    out = jax.ShapeDtypeStruct(task_grad.shape, F32)
    small = (BLOCKS, ROWS, NB)
    return pl.pallas_call(
        kernel,
        out_shape=(out, out),
        in_specs=[any_spec] * 3,
        out_specs=(any_spec, any_spec),
        scratch_shapes=[
            pltpu.VMEM((TOK, DIN), BF),
            pltpu.VMEM((DIN, TOK), BF),
            pltpu.VMEM((TOK, COLS), BF),
            pltpu.VMEM(small, F32),
            pltpu.VMEM(small, F32),
            pltpu.VMEM(small, F32),
            pltpu.VMEM(small, F32),
            pltpu.VMEM(small, BF),
            pltpu.VMEM((BLOCKS, 16, ROWS, NB), BF),
            pltpu.VMEM((BLOCKS, 16, ROWS, NB), BF),
            pltpu.VMEM((BLOCKS, RING, RING, 2, ROWS, NB), BF),
            pltpu.VMEM((TOK, NB), BF),
            pltpu.VMEM((BLOCKS, RING, RING, 2, ROWS, NB), F32),
            pltpu.VMEM((BLOCKS, RING, RING, 2, ROWS, NB), BF),
            pltpu.VMEM((BLOCKS, RING, RING, ROWS, NB), F32),
            pltpu.VMEM((BLOCKS, RING, RING, ROWS, NB), BF),
            pltpu.VMEM((BLOCKS, 16, ROWS, NB), F32),
            pltpu.VMEM((BLOCKS, 16, ROWS, NB), BF),
            pltpu.VMEM((BLOCKS, 3, RING, ROWS, NB), F32),
            pltpu.VMEM((BLOCKS, 3, RING, ROWS, NB), BF),
            pltpu.VMEM((BLOCKS, RING, ROWS, NB), F32),
            pltpu.VMEM((BLOCKS, 3, ROWS, NB), F32),
            pltpu.VMEM((2, 8, 128), F32),
            pltpu.VMEM((2, GROUP, 8, 128), F32),
            pltpu.VMEM((2, 8, 128), F32),
            pltpu.VMEM((2, N_MP, 8, 128), F32),
            pltpu.SemaphoreType.DMA((BLOCKS, 18)),
            pltpu.SemaphoreType.DMA((BLOCKS, 18)),
            pltpu.SemaphoreType.DMA((2, GROUP)),
            pltpu.SemaphoreType.DMA((2, GROUP)),
            pltpu.SemaphoreType.DMA((2, N_MP)),
            pltpu.SemaphoreType.DMA((2, N_MP)),
            pltpu.SemaphoreType.DMA((2 * BLOCKS + 1,)),
        ],
        compiler_params=pltpu.CompilerParams(
            collective_id=0, has_side_effects=True, vmem_limit_bytes=62 * 2**20
        ),
    )(features, curvature, task_grad)


def solution(mesh):
    placed = (P("dp", None), P("dp", "mp"), P("dp", "mp"))
    return jax.shard_map(
        shards,
        mesh=mesh,
        in_specs=placed,
        out_specs=(P("dp", "mp"), P("dp", "mp")),
        check_vma=False,
    )
```

```python
import functools

import jax
import jax.numpy as jnp
from jax import lax
from jax.experimental import pallas as pl
from jax.experimental.pallas import tpu as pltpu
from jax.sharding import PartitionSpec as P

RING = 4
GROUP = 32
N_MP = 4
TOK = 3072
DIN = 1024
COLS = 1024
NB = 256
BLOCKS = COLS // NB
ROWS = DIN // GROUP
TOKENS = 98304.0
DAMP = 0.5
MC = 1536
MESH = pl.DeviceIdType.MESH
BF, F32 = jnp.bfloat16, jnp.float32


def kernel(
    f_h, c_h, g_h, sol_o, res_o,
    f, ft, cv, g, d, w, sol, vb, g_own, g_par, v, wt,
    acc, accb, d0, d0b, s, sb, rin, rinb, t, r2in,
    xsrc, xo, xp, pdv, row, tab, row2, tab2,
    ss, rs, xs, xr, ts, tr, ts2, tr2, ld,
):
    me = lax.axis_index("dp")
    mx = lax.axis_index("mp")
    c = lax.rem(me, 2)
    chip = me // 2
    z = chip // RING
    y = lax.rem(chip, RING)
    pa = (1 - c) * y + c * z
    pb = (1 - c) * z + c * y

    def a_at(k):
        q = lax.rem(pa + k, RING)
        return ((1 - c) * (z * RING + q) + c * (q * RING + y)) * 2 + c

    def b_at(k):
        q = lax.rem(pb + k, RING)
        return ((1 - c) * (q * RING + y) + c * (z * RING + q)) * 2 + c

    partner = me + 1 - 2 * c
    a_up, a_dn, a_op = a_at(1), a_at(3), a_at(2)
    b_up, b_dn, b_op = b_at(1), b_at(3), b_at(2)
    qa_up, qa_dn, qa_op = lax.rem(pa + 1, RING), lax.rem(pa + 3, RING), lax.rem(pa + 2, RING)
    qb_up, qb_dn, qb_op = lax.rem(pb + 1, RING), lax.rem(pb + 3, RING), lax.rem(pb + 2, RING)

    loads = [
        pltpu.make_async_copy(g_h.at[:, pl.ds(j * NB, NB)], g.at[j], ld.at[j])
        for j in range(BLOCKS)
    ]
    parts = 4
    f_loads = [
        pltpu.make_async_copy(
            f_h.at[pl.ds(k * (TOK // parts), TOK // parts)],
            f.at[pl.ds(k * (TOK // parts), TOK // parts)],
            ld.at[BLOCKS + k],
        )
        for k in range(parts)
    ]
    c_load = pltpu.make_async_copy(c_h, cv, ld.at[BLOCKS + parts])
    for x in (*loads, *f_loads, c_load):
        x.start()

    barrier = pltpu.get_barrier_semaphore()

    for q in (a_up, a_dn, a_op, b_up, b_dn, b_op, partner):
        pl.semaphore_signal(barrier, inc=1, device_id={"dp": q}, device_id_type=MESH)

    for k in range(1, N_MP):
        pl.semaphore_signal(
            barrier, inc=1, device_id={"mp": lax.rem(mx + k, N_MP)}, device_id_type=MESH
        )

    def copy(j, i, src, dst, dev):
        return pltpu.make_async_remote_copy(
            src_ref=src, dst_ref=dst, send_sem=ss.at[j, i], recv_sem=rs.at[j, i],
            device_id={"dp": dev}, device_id_type=MESH,
        )

    def send(j, i, src, dst, dev):
        copy(j, i, src, dst, dev).start()

    def got(j, i, dst):
        copy(j, i, dst, dst, partner).wait_recv()

    def sent(j, i, src):
        copy(j, i, src, src, partner).wait_send()

    def strip(buf, j, q):
        return buf.at[j, pl.ds(q * RING, RING)]

    class Gather:
        def __init__(self, src, own, par, sends, recvs):
            self.src, self.own, self.par, self.sends, self.recvs = src, own, par, sends, recvs

        def copy(self, j, i, src, dst, dev):
            return pltpu.make_async_remote_copy(
                src_ref=src, dst_ref=dst, send_sem=self.sends.at[j, i], recv_sem=self.recvs.at[j, i],
                device_id={"dp": dev}, device_id_type=MESH,
            )

        def got(self, j, i, dst):
            self.copy(j, i, dst, dst, partner).wait_recv()

        def first(self, j):
            at = pb * RING + pa
            for i, dev in enumerate((a_up, a_dn, a_op)):
                self.copy(j, i, self.src.at[j], self.own.at[j, at], dev).start()
            self.own[j, at] = self.src[j]

        def second(self, j):
            for i, q in enumerate((qa_dn, qa_up, qa_op)):
                self.got(j, i, self.own.at[j, pb * RING + q])
            mine = strip(self.own, j, pb)
            for i, dev in enumerate((b_up, b_dn, b_op)):
                self.copy(j, 3 + i, mine, mine, dev).start()
            self.copy(j, 6, mine, strip(self.par, j, pb), partner).start()

        def third(self, j):
            for i, q in enumerate((qb_dn, qb_up, qb_op)):
                part = strip(self.own, j, q)
                self.got(j, 3 + i, part)
                self.copy(j, 7 + i, part, strip(self.par, j, q), partner).start()

        def landed(self, j):
            for i, q in enumerate((pa, qa_dn, qa_up, qa_op)):
                self.got(j, 6 + i, strip(self.par, j, q))

        def drain(self, j):
            for i in range(10):
                src = self.src.at[j] if i < 3 else strip(self.own, j, 0)
                self.copy(j, i, src, src, partner).wait_send()

    ag = Gather(vb, g_own, g_par, ss, rs)
    xg = Gather(xsrc, xo, xp, xs, xr)

    def places():
        for zz in range(RING):
            for yy in range(RING):
                zy, yz = zz * RING + yy, yy * RING + zz
                yield zz, yy, (1 - c) * zy + c * yz, (1 - c) * yz + c * zy

    def fill(j):
        ag.landed(j)
        for zz, yy, mine, other in places():
            v[j, zz, yy, c] = g_own[j, mine]
            v[j, zz, yy, 1 - c] = g_par[j, other]

    def local(j, step, beta):
        for zz, yy, mine, other in places():
            for buf, at, core in ((xo, mine, c), (xp, other, 1 - c)):
                gv = buf[j, at]
                nxt = (gv - step * buf[2 + j, at]) + beta * gv
                buf[j, at] = nxt
                v[j, zz, yy, core] = nxt.astype(BF)

    def pd(j, slot):
        part = jnp.zeros((ROWS, NB), F32)
        for zz, yy, mine, other in places():
            part += acc[j, zz, yy, c] * xo[slot, mine] + acc[j, zz, yy, 1 - c] * xp[slot, other]
        pdv[j] = part

    def alone(j):
        return pl.loop(0, (j + BLOCKS) // BLOCKS)

    def p1(j, m):
        r = pl.ds(m * MC, MC)
        cols = pl.ds(pl.multiple_of(j * NB, NB), NB)

        @alone(j)
        def _(_):
            p = jnp.dot(f[r, :], v[j].reshape(DIN, NB), preferred_element_type=F32)
            wt[r, :] = (cv[r, cols].astype(F32) * p).astype(BF)

    def p2(j, h, low):
        r = pl.ds(h * (DIN // 2), DIN // 2)
        zs = pl.ds(2 * h, 2)

        @alone(j)
        def _(_):
            out = jnp.dot(ft[r, :], wt[...], preferred_element_type=F32)
            out = out.reshape(2, RING, 2, ROWS, NB)
            acc[j, zs] = out
            if low:
                accb[j, zs] = out.astype(BF)

        src, dst = (accb, d0b) if low else (acc, d0)
        send(j, 10 + h, src.at[j, zs, :, 1 - c], dst.at[j, zs], partner)

    def r1(j, low):
        src, inn, sm = (d0b, rinb, sb) if low else (d0, rin, s)
        for h in range(2):
            got(j, 10 + h, src.at[j, pl.ds(2 * h, 2)])
            for zz in (2 * h, 2 * h + 1):
                for yy in range(RING):
                    zy, yz = zz * RING + yy, yy * RING + zz
                    both = acc[j, zz, yy, c] + src[j, zz, yy].astype(F32)
                    s[j, (1 - c) * yz + c * zy] = both
                    if low:
                        sb[j, (1 - c) * yz + c * zy] = both.astype(BF)
        send(j, 12, strip(sm, j, qa_up), inn.at[j, 0], a_up)
        send(j, 13, strip(sm, j, qa_dn), inn.at[j, 1], a_dn)
        send(j, 14, strip(sm, j, qa_op), inn.at[j, 2], a_op)

    def r3(j, low):
        inn = rinb if low else rin
        for i in range(3):
            got(j, 12 + i, inn.at[j, i])
        mine = s[j, pl.ds(pa * RING, RING)]
        t[j] = (mine + inn[j, 2].astype(F32)) + (inn[j, 0].astype(F32) + inn[j, 1].astype(F32))
        send(j, 15, t.at[j, qb_up], r2in.at[j, 0], b_up)
        send(j, 16, t.at[j, qb_dn], r2in.at[j, 1], b_dn)
        send(j, 17, t.at[j, qb_op], r2in.at[j, 2], b_op)

    def r4(j):
        for i in range(3):
            got(j, 15 + i, r2in.at[j, i])
        total = (t[j, pb] + r2in[j, 2]) + (r2in[j, 0] + r2in[j, 1])
        w[j] = total / TOKENS + DAMP * d[j]

    def drain(low):
        @pl.loop(0, BLOCKS)
        def _(j):
            for i in (10, 11):
                sent(j, i, (d0b if low else d0).at[j, pl.ds(0, 2)])
            for i in (12, 13, 14):
                sent(j, i, (rinb if low else rin).at[j, 0])
            for i in (15, 16, 17):
                sent(j, i, t.at[j, 0])

    def transpose(k0, k1):
        @pl.loop(k0, k1)
        def _(k):
            r = pl.ds(pl.multiple_of(k * 256, 256), 256)
            ft[:, r] = f[r, :].T

    def operator_first():
        for j in range(BLOCKS):
            vb[j] = d[j].astype(BF)
        for i in range(2):
            xsrc[i] = g[i]
        pl.semaphore_wait(barrier, 7 + N_MP - 1)
        ag.first(0)
        ag.first(1)
        f_loads[0].wait()
        f_loads[1].wait()
        transpose(0, 6)
        ag.second(0)
        ag.first(2)
        ag.first(3)
        ag.second(1)
        xg.first(0)
        xg.first(1)
        f_loads[2].wait()
        f_loads[3].wait()
        transpose(6, 12)
        ag.third(0)
        ag.second(2)
        ag.second(3)
        xg.second(0)
        xg.second(1)
        c_load.wait()
        fill(0)

        @pl.loop(0, BLOCKS)
        def _(j):
            p1(j, 0)

            @pl.when(j < BLOCKS - 1)
            def _():
                ag.third(j + 1)

            @pl.when(j >= 1)
            def _():
                r1(j - 1, False)

            p1(j, 1)

            @pl.when(j >= 2)
            def _():
                r3(j - 2, False)

            p2(j, 0, False)

            @pl.when(j < BLOCKS - 1)
            def _():
                fill(j + 1)

            @pl.when((j >= 1) & (j < 3))
            def _():
                xg.third(j - 1)

            @pl.when(j >= 3)
            def _():
                r4(j - 3)
                xsrc[2] = w[0]
                xg.first(2)

            p2(j, 1, False)

        last = BLOCKS - 1
        r1(last, False)
        r3(last - 1, False)
        r4(last - 2)
        xsrc[3] = w[1]
        xg.first(3)
        r3(last, False)
        xg.second(2)
        r4(last - 1)
        r4(last)

    def operator_second(step, beta):
        for j in (2, 3):
            vb[j] = d[j].astype(BF)
            xsrc[2 + j] = d[j]
        ag.first(2)
        ag.first(3)
        xg.first(4)
        xg.first(5)
        local(0, step, beta)

        @pl.loop(0, BLOCKS)
        def _(j):
            p1(j, 0)

            @pl.when(j >= 1)
            def _():
                r1(j - 1, True)

            p1(j, 1)

            @pl.when(j == 1)
            def _():
                ag.third(2)
                pd(0, 0)

            @pl.when(j == 2)
            def _():
                pd(1, 1)

            @pl.when(j == 3)
            def _():
                xg.third(5)
                xg.landed(4)
                pd(2, 4)

            @pl.when(j >= 2)
            def _():
                r3(j - 2, True)

            p2(j, 0, True)

            @pl.when(j == 0)
            def _():
                local(1, step, beta)
                ag.second(2)
                ag.second(3)

            @pl.when(j == 1)
            def _():
                ag.third(3)

            @pl.when(j == 2)
            def _():
                xg.third(4)
                fill(3)

            @pl.when(j >= 3)
            def _():
                r4(j - 3)

            p2(j, 1, True)

            @pl.when(j == 0)
            def _():
                xg.second(4)
                xg.second(5)

            @pl.when(j == 1)
            def _():
                fill(2)

        last = BLOCKS - 1
        xg.landed(5)
        pd(3, 5)
        dv = d[...]
        exchange_send(1, (total(pdv[...]) / TOKENS + DAMP * total(dv * dv),))
        r1(last, True)
        r3(last - 1, True)
        r4(last - 2)
        r3(last, True)
        exchange_middle(1, lambda tb: (jnp.sum(column(tb, 0), axis=0),))
        r4(last - 1)
        r4(last)

    def total(x):
        return jnp.sum(jnp.sum(jnp.sum(x, axis=0), axis=0, keepdims=True), axis=1, keepdims=True)

    def put(buf, i, values):
        buf[i] = jnp.zeros((8, 128), F32)
        for k, x in enumerate(values):
            buf[i, pl.ds(k, 1), :] = jnp.broadcast_to(x, (1, 128))

    def to_group(turn, k, q):
        return pltpu.make_async_remote_copy(
            src_ref=row.at[turn], dst_ref=tab.at[turn, q],
            send_sem=ts.at[turn, k], recv_sem=tr.at[turn, q],
            device_id={"dp": lax.rem(me + k, GROUP)}, device_id_type=MESH,
        )

    def to_mp(turn, k, q):
        return pltpu.make_async_remote_copy(
            src_ref=row2.at[turn], dst_ref=tab2.at[turn, q],
            send_sem=ts2.at[turn, k], recv_sem=tr2.at[turn, k],
            device_id={"mp": lax.rem(mx + k, N_MP)}, device_id_type=MESH,
        )

    def exchange_send(turn, values):
        put(row, turn, values)

        @pl.loop(1, GROUP)
        def _(k):
            to_group(turn, k, me).start()

        tab[turn, me] = row[turn]

    def exchange_middle(turn, middle):
        @pl.loop(1, GROUP)
        def _(k):
            to_group(turn, k, lax.rem(me + k, GROUP)).wait()

        put(row2, turn, middle(tab[turn]))
        for k in range(1, N_MP):
            to_mp(turn, k, mx).start()
        tab2[turn, mx] = row2[turn]

    def exchange_end(turn):
        for k in range(1, N_MP):
            to_mp(turn, k, lax.rem(mx + N_MP - k, N_MP)).wait()
        return tab2[turn]

    def column(tb, k):
        return tb[:, k : k + 1, :]

    def moved(tb, x):
        ww, uu, uw, at = (column(tb, k) for k in (2, 3, 4, 5))
        gap = at - x
        return jnp.sum(uu + gap * (2.0 * uw + gap * ww), axis=0), jnp.sum(uw + gap * ww, axis=0)

    def ratio(p, q):
        return jnp.where(q > 0, p / jnp.where(q > 0, q, 1.0), 0.0)

    def centre(tb):
        gg, gw, ww = (jnp.sum(column(tb, k), axis=0) for k in range(3))
        x = ratio(gw, ww)
        uu, uw = moved(tb, x)
        return gg, gw, ww, uu, uw, x

    for x in loads:
        x.wait()
    d[...] = g[...]
    operator_first()
    gv, wv = g[...], w[...]
    gg, gw, ww = total(gv * gv), total(gv * wv), total(wv * wv)
    x = ratio(gw, ww)
    u = gv - x * wv
    for j in range(BLOCKS):
        ag.drain(j)
    exchange_send(0, (gg, gw, ww, total(u * u), total(u * wv), x))
    xg.second(3)
    xg.third(2)
    drain(False)
    exchange_middle(0, centre)
    xg.third(3)
    for i in range(4):
        xg.drain(i)
        xg.landed(i)
    tb = exchange_end(0)
    norm = jnp.sum(column(tb, 0), axis=0)
    step = norm / jnp.sum(column(tb, 1), axis=0)
    norm_next, _ = moved(tb, step)
    beta = (norm_next / norm)[:, :1]
    step = step[:, :1]
    sol[...] = step * gv
    res = gv - step * wv
    g[...] = res
    d[...] = res + beta * gv
    operator_second(step, beta)
    tb = exchange_end(1)
    step = (norm_next / jnp.sum(column(tb, 0), axis=0))[:, :1]
    dv, wv = d[...], w[...]
    for j in range(BLOCKS):
        cols = pl.ds(j * NB, NB)
        sol_o[:, cols] = sol[j] + step * dv[j]
        res_o[:, cols] = g[j] - step * wv[j]
    drain(True)
    for j in (2, 3):
        ag.drain(j)
        xg.drain(2 + j)


def shards(features, curvature, task_grad):
    any_spec = pl.BlockSpec(memory_space=pltpu.HBM)
    out = jax.ShapeDtypeStruct(task_grad.shape, F32)
    small = (BLOCKS, ROWS, NB)
    return pl.pallas_call(
        kernel,
        out_shape=(out, out),
        in_specs=[any_spec] * 3,
        out_specs=(pl.BlockSpec(memory_space=pltpu.VMEM),) * 2,
        scratch_shapes=[
            pltpu.VMEM((TOK, DIN), BF),
            pltpu.VMEM((DIN, TOK), BF),
            pltpu.VMEM((TOK, COLS), BF),
            pltpu.VMEM(small, F32),
            pltpu.VMEM(small, F32),
            pltpu.VMEM(small, F32),
            pltpu.VMEM(small, F32),
            pltpu.VMEM(small, BF),
            pltpu.VMEM((BLOCKS, 16, ROWS, NB), BF),
            pltpu.VMEM((BLOCKS, 16, ROWS, NB), BF),
            pltpu.VMEM((BLOCKS, RING, RING, 2, ROWS, NB), BF),
            pltpu.VMEM((TOK, NB), BF),
            pltpu.VMEM((BLOCKS, RING, RING, 2, ROWS, NB), F32),
            pltpu.VMEM((BLOCKS, RING, RING, 2, ROWS, NB), BF),
            pltpu.VMEM((BLOCKS, RING, RING, ROWS, NB), F32),
            pltpu.VMEM((BLOCKS, RING, RING, ROWS, NB), BF),
            pltpu.VMEM((BLOCKS, 16, ROWS, NB), F32),
            pltpu.VMEM((BLOCKS, 16, ROWS, NB), BF),
            pltpu.VMEM((BLOCKS, 3, RING, ROWS, NB), F32),
            pltpu.VMEM((BLOCKS, 3, RING, ROWS, NB), BF),
            pltpu.VMEM((BLOCKS, RING, ROWS, NB), F32),
            pltpu.VMEM((BLOCKS, 3, ROWS, NB), F32),
            pltpu.VMEM((6, ROWS, NB), F32),
            pltpu.VMEM((6, 16, ROWS, NB), F32),
            pltpu.VMEM((6, 16, ROWS, NB), F32),
            pltpu.VMEM(small, F32),
            pltpu.VMEM((2, 8, 128), F32),
            pltpu.VMEM((2, GROUP, 8, 128), F32),
            pltpu.VMEM((2, 8, 128), F32),
            pltpu.VMEM((2, N_MP, 8, 128), F32),
            pltpu.SemaphoreType.DMA((BLOCKS, 18)),
            pltpu.SemaphoreType.DMA((BLOCKS, 18)),
            pltpu.SemaphoreType.DMA((6, 10)),
            pltpu.SemaphoreType.DMA((6, 10)),
            pltpu.SemaphoreType.DMA((2, GROUP)),
            pltpu.SemaphoreType.DMA((2, GROUP)),
            pltpu.SemaphoreType.DMA((2, N_MP)),
            pltpu.SemaphoreType.DMA((2, N_MP)),
            pltpu.SemaphoreType.DMA((2 * BLOCKS + 1,)),
        ],
        compiler_params=pltpu.CompilerParams(
            collective_id=0, has_side_effects=True, vmem_limit_bytes=51 * 2**20
        ),
    )(features, curvature, pltpu.with_memory_space_constraint(task_grad, pltpu.HBM))


def solution(mesh):
    placed = (P("dp", None), P("dp", "mp"), P("dp", "mp"))
    return jax.shard_map(
        shards,
        mesh=mesh,
        in_specs=placed,
        out_specs=(P("dp", "mp"), P("dp", "mp")),
        check_vma=False,
    )
```

```python
import functools

import jax
import jax.numpy as jnp
from jax import lax
from jax.experimental import pallas as pl
from jax.experimental.pallas import tpu as pltpu
from jax.sharding import PartitionSpec as P

RING = 4
GROUP = 32
N_MP = 4
TOK = 3072
DIN = 1024
COLS = 1024
NB = 256
BLOCKS = COLS // NB
ROWS = DIN // GROUP
TOKENS = 98304.0
DAMP = 0.5
MESH = pl.DeviceIdType.MESH
BF, F32 = jnp.bfloat16, jnp.float32
FAR_FIRST = sorted(
    ((i, k) for i in range(RING) for k in range(RING) if i or k),
    key=lambda t: -min(t[0], RING - t[0]) - min(t[1], RING - t[1]),
)


def kernel(
    f_h, c_h, g_h, sol_o, res_o,
    f, ft, cv, g, d, w, sol, vb, g_own, g_par, v, wt,
    acc, accb, d0, d0b, s, sb, rin, t, r2in,
    din, xsrc, xo, xp, lsrc, lo, lp, pdv, row, tab, one_row, one_tab, row2, tab2,
    ss, rs, xs, xr, ls, lr, ds, dr, ts, tr, ts2, tr2, ld,
):
    me = lax.axis_index("dp")
    mx = lax.axis_index("mp")
    c = lax.rem(me, 2)
    chip = me // 2
    z = chip // RING
    y = lax.rem(chip, RING)
    pa = (1 - c) * y + c * z
    pb = (1 - c) * z + c * y

    def a_at(k):
        q = lax.rem(pa + k, RING)
        return ((1 - c) * (z * RING + q) + c * (q * RING + y)) * 2 + c

    def b_at(k):
        q = lax.rem(pb + k, RING)
        return ((1 - c) * (q * RING + y) + c * (z * RING + q)) * 2 + c

    partner = me + 1 - 2 * c
    a_up, a_dn, a_op = a_at(1), a_at(3), a_at(2)
    b_up, b_dn, b_op = b_at(1), b_at(3), b_at(2)
    qa_up, qa_dn, qa_op = lax.rem(pa + 1, RING), lax.rem(pa + 3, RING), lax.rem(pa + 2, RING)
    qb_up, qb_dn, qb_op = lax.rem(pb + 1, RING), lax.rem(pb + 3, RING), lax.rem(pb + 2, RING)

    loads = [
        pltpu.make_async_copy(g_h.at[:, pl.ds(j * NB, NB)], g.at[j], ld.at[j])
        for j in range(BLOCKS)
    ]
    parts = 4
    f_loads = [
        pltpu.make_async_copy(
            f_h.at[pl.ds(k * (TOK // parts), TOK // parts)],
            f.at[pl.ds(k * (TOK // parts), TOK // parts)],
            ld.at[BLOCKS + k],
        )
        for k in range(parts)
    ]
    c_load = pltpu.make_async_copy(c_h, cv, ld.at[BLOCKS + parts])
    for x in (*loads, *f_loads, c_load):
        x.start()

    barrier = pltpu.get_barrier_semaphore()

    for q in (a_up, a_dn, a_op, b_up, b_dn, b_op, partner):
        pl.semaphore_signal(barrier, inc=1, device_id={"dp": q}, device_id_type=MESH)

    for k in range(1, N_MP):
        pl.semaphore_signal(
            barrier, inc=1, device_id={"mp": lax.rem(mx + k, N_MP)}, device_id_type=MESH
        )

    def copy(j, i, src, dst, dev):
        return pltpu.make_async_remote_copy(
            src_ref=src, dst_ref=dst, send_sem=ss.at[j, i], recv_sem=rs.at[j, i],
            device_id={"dp": dev}, device_id_type=MESH,
        )

    def send(j, i, src, dst, dev):
        copy(j, i, src, dst, dev).start()

    def got(j, i, dst):
        copy(j, i, dst, dst, partner).wait_recv()

    def sent(j, i, src):
        copy(j, i, src, src, partner).wait_send()

    def strip(buf, j, q):
        return buf.at[j, pl.ds(q * RING, RING)]

    class Gather:
        def __init__(self, src, own, par, sends, recvs):
            self.src, self.own, self.par, self.sends, self.recvs = src, own, par, sends, recvs

        def copy(self, j, i, src, dst, dev):
            return pltpu.make_async_remote_copy(
                src_ref=src, dst_ref=dst, send_sem=self.sends.at[j, i], recv_sem=self.recvs.at[j, i],
                device_id={"dp": dev}, device_id_type=MESH,
            )

        def got(self, j, i, dst):
            self.copy(j, i, dst, dst, partner).wait_recv()

        def first(self, j):
            at = pb * RING + pa
            for i, dev in enumerate((a_up, a_dn, a_op)):
                self.copy(j, i, self.src.at[j], self.own.at[j, at], dev).start()
            self.own[j, at] = self.src[j]

        def second(self, j):
            for i, q in enumerate((qa_dn, qa_up, qa_op)):
                self.got(j, i, self.own.at[j, pb * RING + q])
            mine = strip(self.own, j, pb)
            for i, dev in enumerate((b_up, b_dn, b_op)):
                self.copy(j, 3 + i, mine, mine, dev).start()
            self.copy(j, 6, mine, strip(self.par, j, pb), partner).start()

        def third(self, j):
            for i, q in enumerate((qb_dn, qb_up, qb_op)):
                part = strip(self.own, j, q)
                self.got(j, 3 + i, part)
                self.copy(j, 7 + i, part, strip(self.par, j, q), partner).start()

        def landed(self, j):
            for i, q in enumerate((pa, qa_dn, qa_up, qa_op)):
                self.got(j, 6 + i, strip(self.par, j, q))

        def drain(self, j):
            for i in range(10):
                src = self.src.at[j] if i < 3 else strip(self.own, j, 0)
                self.copy(j, i, src, src, partner).wait_send()

    ag = Gather(vb, g_own, g_par, ss, rs)
    xg = Gather(xsrc, xo, xp, xs, xr)
    lg = Gather(lsrc, lo, lp, ls, lr)

    def places():
        for zz in range(RING):
            for yy in range(RING):
                zy, yz = zz * RING + yy, yy * RING + zz
                yield zz, yy, (1 - c) * zy + c * yz, (1 - c) * yz + c * zy

    def fill(j):
        ag.landed(j)
        for zz, yy, mine, other in places():
            v[j, zz, yy, c] = g_own[j, mine]
            v[j, zz, yy, 1 - c] = g_par[j, other]

    def local(j, step, beta):
        for zz, yy, mine, other in places():
            for buf, at, core in ((xo, mine, c), (xp, other, 1 - c)):
                gv = buf[j, at]
                nxt = (gv - step * buf[2 + j, at]) + beta * gv
                buf[j, at] = nxt
                v[j, zz, yy, core] = nxt.astype(BF)

    def pd(j):
        part = jnp.zeros((ROWS, NB), F32)
        for zz, yy, mine, other in places():
            part += acc[j, zz, yy, c] * xo[j, mine] + acc[j, zz, yy, 1 - c] * xp[j, other]
        pdv[j] = part

    def pd_rest(j):
        part = jnp.zeros((ROWS, NB), F32)
        for zz, yy, mine, other in places():
            for core, rest in ((c, lo[j - 2, mine]), (1 - c, lp[j - 2, other])):
                part += acc[j, zz, yy, core] * (v[j, zz, yy, core].astype(F32) + rest.astype(F32))
        pdv[j] = part

    def alone(j):
        return pl.loop(0, (j + BLOCKS) // BLOCKS)

    def p1(j):
        cols = pl.ds(pl.multiple_of(j * NB, NB), NB)

        @alone(j)
        def _(_):
            p = jnp.dot(f[...], v[j].reshape(DIN, NB), preferred_element_type=F32)
            wt[...] = (cv[:, cols].astype(F32) * p).astype(BF)

    def p2(j, h, low):
        r = pl.ds(h * (DIN // 2), DIN // 2)
        zs = pl.ds(2 * h, 2)

        @alone(j)
        def _(_):
            out = jnp.dot(ft[r, :], wt[...], preferred_element_type=F32)
            out = out.reshape(2, RING, 2, ROWS, NB)
            acc[j, zs] = out
            if low:
                accb[j, zs] = out.astype(BF)

        src, dst = (accb, d0b) if low else (acc, d0)
        send(j, 10 + h, src.at[j, zs, :, 1 - c], dst.at[j, zs], partner)

    def r1(j, low):
        src = d0b if low else d0
        for h in range(2):
            got(j, 10 + h, src.at[j, pl.ds(2 * h, 2)])
            for zz in (2 * h, 2 * h + 1):
                for yy in range(RING):
                    zy, yz = zz * RING + yy, yy * RING + zz
                    both = acc[j, zz, yy, c] + src[j, zz, yy].astype(F32)
                    s[j, (1 - c) * yz + c * zy] = both
                    if low:
                        sb[j, (1 - c) * yz + c * zy] = both.astype(BF)
        if low:
            for ka, kb in FAR_FIRST:
                piece(j, ka, kb).start()
        else:
            send(j, 12, strip(s, j, qa_up), rin.at[j, 0], a_up)
            send(j, 13, strip(s, j, qa_dn), rin.at[j, 1], a_dn)
            send(j, 14, strip(s, j, qa_op), rin.at[j, 2], a_op)

    def piece(j, ka, kb):
        qa, qb = lax.rem(pa + ka, RING), lax.rem(pb + kb, RING)
        dev = ((1 - c) * (qb * RING + qa) + c * (qa * RING + qb)) * 2 + c
        return pltpu.make_async_remote_copy(
            src_ref=sb.at[j, qa * RING + qb], dst_ref=din.at[j, ka * RING + kb],
            send_sem=ds.at[j, ka * RING + kb], recv_sem=dr.at[j, ka * RING + kb],
            device_id={"dp": dev}, device_id_type=MESH,
        )

    def r4_low(j):
        total = s[j, pa * RING + pb]
        for ka, kb in reversed(FAR_FIRST):
            piece(j, ka, kb).wait_recv()
            total += din[j, ka * RING + kb].astype(F32)
        w[j] = total / TOKENS + DAMP * d[j]

    def r3(j):
        for i in range(3):
            got(j, 12 + i, rin.at[j, i])
        mine = s[j, pl.ds(pa * RING, RING)]
        t[j] = (mine + rin[j, 2]) + (rin[j, 0] + rin[j, 1])
        send(j, 15, t.at[j, qb_up], r2in.at[j, 0], b_up)
        send(j, 16, t.at[j, qb_dn], r2in.at[j, 1], b_dn)
        send(j, 17, t.at[j, qb_op], r2in.at[j, 2], b_op)

    def r4(j):
        for i in range(3):
            got(j, 15 + i, r2in.at[j, i])
        total = (t[j, pb] + r2in[j, 2]) + (r2in[j, 0] + r2in[j, 1])
        w[j] = total / TOKENS + DAMP * d[j]

    def drain(low):
        @pl.loop(0, BLOCKS)
        def _(j):
            for i in (10, 11):
                sent(j, i, (d0b if low else d0).at[j, pl.ds(0, 2)])
            if low:
                for ka, kb in FAR_FIRST:
                    piece(j, ka, kb).wait_send()
            else:
                for i in (12, 13, 14):
                    sent(j, i, rin.at[j, 0])
                for i in (15, 16, 17):
                    sent(j, i, t.at[j, 0])

    def transpose(k0, k1):
        @pl.loop(k0, k1)
        def _(k):
            r = pl.ds(pl.multiple_of(k * 256, 256), 256)
            ft[:, r] = f[r, :].T

    def operator_first():
        for j in range(BLOCKS):
            vb[j] = d[j].astype(BF)
        for i in range(2):
            xsrc[i] = g[i]
        pl.semaphore_wait(barrier, 7 + N_MP - 1)
        ag.first(0)
        ag.first(1)
        f_loads[0].wait()
        f_loads[1].wait()
        transpose(0, 6)
        ag.second(0)
        ag.first(2)
        ag.first(3)
        ag.second(1)
        xg.first(0)
        xg.first(1)
        f_loads[2].wait()
        f_loads[3].wait()
        transpose(6, 12)
        ag.third(0)
        ag.second(2)
        ag.second(3)
        c_load.wait()
        fill(0)

        @pl.loop(0, BLOCKS)
        def _(j):
            p1(j)

            @pl.when(j < BLOCKS - 1)
            def _():
                ag.third(j + 1)

            @pl.when(j >= 1)
            def _():
                r1(j - 1, False)

            @pl.when(j == 0)
            def _():
                xg.second(0)
                xg.second(1)

            p2(j, 0, False)

            @pl.when(j >= 2)
            def _():
                r3(j - 2)

            @pl.when(j < BLOCKS - 1)
            def _():
                fill(j + 1)

            @pl.when((j >= 1) & (j < 3))
            def _():
                xg.third(j - 1)

            @pl.when(j >= 3)
            def _():
                r4(j - 3)
                xsrc[2] = w[0]
                xg.first(2)

            p2(j, 1, False)

        last = BLOCKS - 1
        r1(last, False)
        r3(last - 1)
        r4(last - 2)
        xsrc[3] = w[1]
        xg.first(3)
        r3(last)
        xg.second(2)
        r4(last - 1)
        r4(last)

    def operator_second(step, beta):
        for j in (2, 3):
            near = d[j].astype(BF)
            vb[j] = near
            lsrc[j - 2] = (d[j] - near.astype(F32)).astype(BF)
        ag.first(2)
        ag.first(3)
        lg.first(0)
        lg.first(1)
        local(0, step, beta)

        @pl.loop(0, BLOCKS)
        def _(j):
            p1(j)

            @pl.when(j == 0)
            def _():
                xg.third(3)

            @pl.when(j == 1)
            def _():
                ag.third(2)
                pd(0)

            @pl.when(j == 2)
            def _():
                pd(1)

            @pl.when(j == 3)
            def _():
                lg.third(1)
                lg.landed(0)
                pd_rest(2)

            @pl.when(j >= 1)
            def _():
                r1(j - 1, True)

            p2(j, 0, True)

            @pl.when(j == 0)
            def _():
                xg.drain(1)
                xg.landed(1)
                xg.landed(3)
                ag.second(2)
                ag.second(3)
                local(1, step, beta)

            @pl.when(j == 1)
            def _():
                ag.third(3)

            @pl.when(j == 2)
            def _():
                lg.third(0)
                fill(3)

            @pl.when(j >= 3)
            def _():
                r4_low(j - 3)

            p2(j, 1, True)

            @pl.when(j == 0)
            def _():
                lg.second(0)
                lg.second(1)

            @pl.when(j == 1)
            def _():
                fill(2)

        last = BLOCKS - 1
        lg.landed(1)
        pd_rest(3)
        dv = d[...]
        value = total(pdv[...]) / TOKENS + DAMP * total(dv * dv)
        one_row[...] = jnp.broadcast_to(value, (1, 128))

        @pl.loop(1, GROUP)
        def _(k):
            one_to_group(k, me).start()

        one_tab[me] = one_row[...]
        r1(last, True)
        r4_low(last - 2)

        @pl.loop(1, GROUP)
        def _(k):
            one_to_group(k, lax.rem(me + k, GROUP)).wait()

        put(row2.at[1], (jnp.sum(one_tab[...], axis=0),))
        exchange_over_mp(1)
        r4_low(last - 1)
        r4_low(last)

    def total(x):
        return jnp.sum(jnp.sum(jnp.sum(x, axis=0), axis=0, keepdims=True), axis=1, keepdims=True)

    def put(buf, values):
        buf[...] = jnp.zeros((8, 128), F32)
        for k, x in enumerate(values):
            buf[pl.ds(k, 1), :] = jnp.broadcast_to(x, (1, 128))

    def to_group(k, q):
        return pltpu.make_async_remote_copy(
            src_ref=row, dst_ref=tab.at[q], send_sem=ts.at[0, k], recv_sem=tr.at[0, q],
            device_id={"dp": lax.rem(me + k, GROUP)}, device_id_type=MESH,
        )

    def one_to_group(k, q):
        return pltpu.make_async_remote_copy(
            src_ref=one_row, dst_ref=one_tab.at[q], send_sem=ts.at[1, k], recv_sem=tr.at[1, q],
            device_id={"dp": lax.rem(me + k, GROUP)}, device_id_type=MESH,
        )

    def to_mp(turn, k, q):
        return pltpu.make_async_remote_copy(
            src_ref=row2.at[turn], dst_ref=tab2.at[turn, q],
            send_sem=ts2.at[turn, k], recv_sem=tr2.at[turn, k],
            device_id={"mp": lax.rem(mx + k, N_MP)}, device_id_type=MESH,
        )

    def exchange_send(values):
        put(row, values)

        @pl.loop(1, GROUP)
        def _(k):
            to_group(k, me).start()

        tab[me] = row[...]

    def exchange_middle():
        @pl.loop(1, GROUP)
        def _(k):
            to_group(k, lax.rem(me + k, GROUP)).wait()

        put(row2.at[0], centre(tab[...]))
        exchange_over_mp(0)

    def exchange_over_mp(turn):
        for k in range(1, N_MP):
            to_mp(turn, k, mx).start()
        tab2[turn, mx] = row2[turn]

    def exchange_end(turn):
        for k in range(1, N_MP):
            to_mp(turn, k, lax.rem(mx + N_MP - k, N_MP)).wait()
        return tab2[turn]

    def column(tb, k):
        return tb[:, k : k + 1, :]

    def moved(tb, x):
        ww, uu, uw, at = (column(tb, k) for k in (2, 3, 4, 5))
        gap = at - x
        return jnp.sum(uu + gap * (2.0 * uw + gap * ww), axis=0), jnp.sum(uw + gap * ww, axis=0)

    def ratio(p, q):
        return jnp.where(q > 0, p / jnp.where(q > 0, q, 1.0), 0.0)

    def centre(tb):
        gg, gw, ww = (jnp.sum(column(tb, k), axis=0) for k in range(3))
        x = ratio(gw, ww)
        uu, uw = moved(tb, x)
        return gg, gw, ww, uu, uw, x

    for x in loads:
        x.wait()
    d[...] = g[...]
    operator_first()
    gv, wv = g[...], w[...]
    gg, gw, ww = total(gv * gv), total(gv * wv), total(wv * wv)
    x = ratio(gw, ww)
    u = gv - x * wv
    for j in range(BLOCKS):
        ag.drain(j)
    exchange_send((gg, gw, ww, total(u * u), total(u * wv), x))
    xg.second(3)
    xg.third(2)
    drain(False)
    exchange_middle()
    xg.drain(0)
    xg.landed(0)
    xg.landed(2)
    tb = exchange_end(0)
    norm = jnp.sum(column(tb, 0), axis=0)
    step = norm / jnp.sum(column(tb, 1), axis=0)
    norm_next, _ = moved(tb, step)
    beta = (norm_next / norm)[:, :1]
    step = step[:, :1]
    sol[...] = step * gv
    res = gv - step * wv
    g[...] = res
    d[...] = res + beta * gv
    operator_second(step, beta)
    tb = exchange_end(1)
    step = (norm_next / jnp.sum(column(tb, 0), axis=0))[:, :1]
    dv, wv = d[...], w[...]
    for j in range(BLOCKS):
        cols = pl.ds(j * NB, NB)
        sol_o[:, cols] = sol[j] + step * dv[j]
        res_o[:, cols] = g[j] - step * wv[j]
    drain(True)
    for j in (2, 3):
        ag.drain(j)
        xg.drain(j)
        lg.drain(j - 2)


def shards(features, curvature, task_grad):
    any_spec = pl.BlockSpec(memory_space=pltpu.HBM)
    out = jax.ShapeDtypeStruct(task_grad.shape, F32)
    small = (BLOCKS, ROWS, NB)
    return pl.pallas_call(
        kernel,
        out_shape=(out, out),
        in_specs=[any_spec] * 3,
        out_specs=(pl.BlockSpec(memory_space=pltpu.VMEM),) * 2,
        scratch_shapes=[
            pltpu.VMEM((TOK, DIN), BF),
            pltpu.VMEM((DIN, TOK), BF),
            pltpu.VMEM((TOK, COLS), BF),
            pltpu.VMEM(small, F32),
            pltpu.VMEM(small, F32),
            pltpu.VMEM(small, F32),
            pltpu.VMEM(small, F32),
            pltpu.VMEM(small, BF),
            pltpu.VMEM((BLOCKS, 16, ROWS, NB), BF),
            pltpu.VMEM((BLOCKS, 16, ROWS, NB), BF),
            pltpu.VMEM((BLOCKS, RING, RING, 2, ROWS, NB), BF),
            pltpu.VMEM((TOK, NB), BF),
            pltpu.VMEM((BLOCKS, RING, RING, 2, ROWS, NB), F32),
            pltpu.VMEM((BLOCKS, RING, RING, 2, ROWS, NB), BF),
            pltpu.VMEM((BLOCKS, RING, RING, ROWS, NB), F32),
            pltpu.VMEM((BLOCKS, RING, RING, ROWS, NB), BF),
            pltpu.VMEM((BLOCKS, 16, ROWS, NB), F32),
            pltpu.VMEM((BLOCKS, 16, ROWS, NB), BF),
            pltpu.VMEM((BLOCKS, 3, RING, ROWS, NB), F32),
            pltpu.VMEM((BLOCKS, RING, ROWS, NB), F32),
            pltpu.VMEM((BLOCKS, 3, ROWS, NB), F32),
            pltpu.VMEM((BLOCKS, 16, ROWS, NB), BF),
            pltpu.VMEM((4, ROWS, NB), F32),
            pltpu.VMEM((4, 16, ROWS, NB), F32),
            pltpu.VMEM((4, 16, ROWS, NB), F32),
            pltpu.VMEM((2, ROWS, NB), BF),
            pltpu.VMEM((2, 16, ROWS, NB), BF),
            pltpu.VMEM((2, 16, ROWS, NB), BF),
            pltpu.VMEM(small, F32),
            pltpu.VMEM((8, 128), F32),
            pltpu.VMEM((GROUP, 8, 128), F32),
            pltpu.VMEM((1, 128), F32),
            pltpu.VMEM((GROUP, 1, 128), F32),
            pltpu.VMEM((2, 8, 128), F32),
            pltpu.VMEM((2, N_MP, 8, 128), F32),
            pltpu.SemaphoreType.DMA((BLOCKS, 18)),
            pltpu.SemaphoreType.DMA((BLOCKS, 18)),
            pltpu.SemaphoreType.DMA((4, 10)),
            pltpu.SemaphoreType.DMA((4, 10)),
            pltpu.SemaphoreType.DMA((2, 10)),
            pltpu.SemaphoreType.DMA((2, 10)),
            pltpu.SemaphoreType.DMA((BLOCKS, 16)),
            pltpu.SemaphoreType.DMA((BLOCKS, 16)),
            pltpu.SemaphoreType.DMA((2, GROUP)),
            pltpu.SemaphoreType.DMA((2, GROUP)),
            pltpu.SemaphoreType.DMA((2, N_MP)),
            pltpu.SemaphoreType.DMA((2, N_MP)),
            pltpu.SemaphoreType.DMA((2 * BLOCKS + 1,)),
        ],
        compiler_params=pltpu.CompilerParams(
            collective_id=0, has_side_effects=True, vmem_limit_bytes=51 * 2**20
        ),
    )(features, curvature, pltpu.with_memory_space_constraint(task_grad, pltpu.HBM))


def solution(mesh):
    placed = (P("dp", None), P("dp", "mp"), P("dp", "mp"))
    return jax.shard_map(
        shards,
        mesh=mesh,
        in_specs=placed,
        out_specs=(P("dp", "mp"), P("dp", "mp")),
        check_vma=False,
    )
```

```python
import functools

import jax
import jax.numpy as jnp
from jax import lax
from jax.experimental import pallas as pl
from jax.experimental.pallas import tpu as pltpu
from jax.sharding import PartitionSpec as P

RING = 4
GROUP = 32
N_MP = 4
TOK = 3072
DIN = 1024
COLS = 1024
NB = 256
BLOCKS = COLS // NB
ROWS = DIN // GROUP
TOKENS = 98304.0
DAMP = 0.5
MESH = pl.DeviceIdType.MESH
BF, F32 = jnp.bfloat16, jnp.float32
FAR_FIRST = sorted(
    ((i, k) for i in range(RING) for k in range(RING) if i or k),
    key=lambda t: -min(t[0], RING - t[0]) - min(t[1], RING - t[1]),
)


def kernel(
    f_h, c_h, g_h, sol_o, res_o,
    f, ft, cv, g, d, w, sol, vb, g_own, g_par, v, wt,
    acc, accb, d0, d0b, s, sb, rin, t, r2in,
    din, xsrc, xo, xp, lsrc, lo, lp, pdv, row, tab, one_row, one_tab, row2, tab2,
    gs, gr, qs, qr, es, er, ld,
):
    me = lax.axis_index("dp")
    mx = lax.axis_index("mp")
    c = lax.rem(me, 2)
    chip = me // 2
    z = chip // RING
    y = lax.rem(chip, RING)
    pa = (1 - c) * y + c * z
    pb = (1 - c) * z + c * y

    def a_at(k):
        q = lax.rem(pa + k, RING)
        return ((1 - c) * (z * RING + q) + c * (q * RING + y)) * 2 + c

    def b_at(k):
        q = lax.rem(pb + k, RING)
        return ((1 - c) * (q * RING + y) + c * (z * RING + q)) * 2 + c

    partner = me + 1 - 2 * c
    a_up, a_dn, a_op = a_at(1), a_at(3), a_at(2)
    b_up, b_dn, b_op = b_at(1), b_at(3), b_at(2)
    qa_up, qa_dn, qa_op = lax.rem(pa + 1, RING), lax.rem(pa + 3, RING), lax.rem(pa + 2, RING)
    qb_up, qb_dn, qb_op = lax.rem(pb + 1, RING), lax.rem(pb + 3, RING), lax.rem(pb + 2, RING)

    loads = [
        pltpu.make_async_copy(g_h.at[:, pl.ds(j * NB, NB)], g.at[j], ld.at[0])
        for j in range(BLOCKS)
    ]
    parts = 4
    f_loads = [
        pltpu.make_async_copy(
            f_h.at[pl.ds(k * (TOK // parts), TOK // parts)],
            f.at[pl.ds(k * (TOK // parts), TOK // parts)],
            ld.at[1 + k],
        )
        for k in range(parts)
    ]
    c_load = pltpu.make_async_copy(c_h, cv, ld.at[1 + parts])
    for x in (*loads, *f_loads, c_load):
        x.start()

    barrier = pltpu.get_barrier_semaphore()

    for q in (a_up, a_dn, a_op, b_up, b_dn, b_op, partner):
        pl.semaphore_signal(barrier, inc=1, device_id={"dp": q}, device_id_type=MESH)

    for k in range(1, N_MP):
        pl.semaphore_signal(
            barrier, inc=1, device_id={"mp": lax.rem(mx + k, N_MP)}, device_id_type=MESH
        )

    def copy(src, dst, sends, recvs, dev):
        return pltpu.make_async_remote_copy(
            src_ref=src, dst_ref=dst, send_sem=sends, recv_sem=recvs,
            device_id={"dp": dev}, device_id_type=MESH,
        )

    def send(j, i, src, dst, dev):
        copy(src, dst, qs.at[j, i], qr.at[j, i], dev).start()

    def got(j, i, whole):
        copy(whole, whole, qs.at[j, i], qr.at[j, i], partner).wait_recv()

    def sent(j, i, whole):
        copy(whole, whole, qs.at[j, i], qr.at[j, i], partner).wait_send()

    def strip(buf, j, q):
        return buf.at[j, pl.ds(q * RING, RING)]

    class Gather:
        def __init__(self, src, own, par, base):
            self.src, self.own, self.par, self.base = src, own, par, base

        def copy(self, j, i, src, dst, dev):
            return copy(src, dst, gs.at[self.base + j, i], gr.at[self.base + j, i], dev)

        def got(self, j, i, pieces):
            part = self.own.at[j, pl.ds(0, pieces)]
            self.copy(j, i, part, part, partner).wait_recv()

        def first(self, j):
            at = pb * RING + pa
            for dev in (a_up, a_dn, a_op):
                self.copy(j, 0, self.src.at[j], self.own.at[j, at], dev).start()
            self.own[j, at] = self.src[j]

        def second(self, j):
            self.got(j, 0, 3)
            mine = strip(self.own, j, pb)
            for dev in (b_up, b_dn, b_op):
                self.copy(j, 1, mine, mine, dev).start()
            self.copy(j, 2, mine, strip(self.par, j, pb), partner).start()

        def third(self, j):
            self.got(j, 1, 12)
            for q in (qb_dn, qb_up, qb_op):
                self.copy(j, 2, strip(self.own, j, q), strip(self.par, j, q), partner).start()

        def landed(self, j):
            self.got(j, 2, 16)

        def drain(self, j):
            for i, pieces in enumerate((3, 12, 16)):
                part = self.own.at[j, pl.ds(0, pieces)]
                self.copy(j, i, part, part, partner).wait_send()

    ag = Gather(vb, g_own, g_par, 0)
    xg = Gather(xsrc, xo, xp, BLOCKS)
    lg = Gather(lsrc, lo, lp, BLOCKS + 4)

    def places():
        for zz in range(RING):
            for yy in range(RING):
                zy, yz = zz * RING + yy, yy * RING + zz
                yield zz, yy, (1 - c) * zy + c * yz, (1 - c) * yz + c * zy

    def fill(j):
        ag.landed(j)
        for zz, yy, mine, other in places():
            v[j, zz, yy, c] = g_own[j, mine]
            v[j, zz, yy, 1 - c] = g_par[j, other]

    def local(j, step, beta):
        for zz, yy, mine, other in places():
            for buf, at, core in ((xo, mine, c), (xp, other, 1 - c)):
                gv = buf[j, at]
                nxt = (gv - step * buf[2 + j, at]) + beta * gv
                buf[j, at] = nxt
                v[j, zz, yy, core] = nxt.astype(BF)

    def pd(j):
        part = jnp.zeros((ROWS, NB), F32)
        for zz, yy, mine, other in places():
            part += acc[j, zz, yy, c] * xo[j, mine] + acc[j, zz, yy, 1 - c] * xp[j, other]
        pdv[j] = part

    def pd_rest(j):
        part = jnp.zeros((ROWS, NB), F32)
        for zz, yy, mine, other in places():
            for core, rest in ((c, lo[j - 2, mine]), (1 - c, lp[j - 2, other])):
                part += acc[j, zz, yy, core] * (v[j, zz, yy, core].astype(F32) + rest.astype(F32))
        pdv[j] = part

    def alone(j):
        return pl.loop(0, (j + BLOCKS) // BLOCKS)

    def p1(j):
        cols = pl.ds(pl.multiple_of(j * NB, NB), NB)

        @alone(j)
        def _(_):
            p = jnp.dot(f[...], v[j].reshape(DIN, NB), preferred_element_type=F32)
            wt[...] = (cv[:, cols].astype(F32) * p).astype(BF)

    def p2(j, h, low):
        r = pl.ds(h * (DIN // 2), DIN // 2)
        zs = pl.ds(2 * h, 2)

        @alone(j)
        def _(_):
            out = jnp.dot(ft[r, :], wt[...], preferred_element_type=F32)
            out = out.reshape(2, RING, 2, ROWS, NB)
            acc[j, zs] = out
            if low:
                accb[j, zs] = out.astype(BF)

        src, dst = (accb, d0b) if low else (acc, d0)
        send(j, 0, src.at[j, zs, :, 1 - c], dst.at[j, zs], partner)

    def r1(j, low):
        src = d0b if low else d0
        got(j, 0, src.at[j])
        for zz, yy, _, at in places():
            both = acc[j, zz, yy, c] + src[j, zz, yy].astype(F32)
            s[j, at] = both
            if low:
                sb[j, at] = both.astype(BF)
        if low:
            for ka, kb in FAR_FIRST:
                piece(j, ka, kb)
        else:
            send(j, 1, strip(s, j, qa_up), rin.at[j, 0], a_up)
            send(j, 1, strip(s, j, qa_dn), rin.at[j, 1], a_dn)
            send(j, 1, strip(s, j, qa_op), rin.at[j, 2], a_op)

    def piece(j, ka, kb):
        qa, qb = lax.rem(pa + ka, RING), lax.rem(pb + kb, RING)
        dev = ((1 - c) * (qb * RING + qa) + c * (qa * RING + qb)) * 2 + c
        send(j, 3, sb.at[j, qa * RING + qb], din.at[j, ka * RING + kb], dev)

    def r4_low(j):
        got(j, 3, din.at[j, pl.ds(1, 15)])
        total = s[j, pa * RING + pb]
        for k in range(1, 16):
            total += din[j, k].astype(F32)
        w[j] = total / TOKENS + DAMP * d[j]

    def r3(j):
        got(j, 1, rin.at[j])
        mine = s[j, pl.ds(pa * RING, RING)]
        t[j] = (mine + rin[j, 2]) + (rin[j, 0] + rin[j, 1])
        send(j, 2, t.at[j, qb_up], r2in.at[j, 0], b_up)
        send(j, 2, t.at[j, qb_dn], r2in.at[j, 1], b_dn)
        send(j, 2, t.at[j, qb_op], r2in.at[j, 2], b_op)

    def r4(j):
        got(j, 2, r2in.at[j])
        total = (t[j, pb] + r2in[j, 2]) + (r2in[j, 0] + r2in[j, 1])
        w[j] = total / TOKENS + DAMP * d[j]

    def drain(low):
        for j in range(BLOCKS):
            sent(j, 0, (d0b if low else d0).at[j])
            if low:
                sent(j, 3, din.at[j, pl.ds(1, 15)])
            else:
                sent(j, 1, rin.at[j])
                sent(j, 2, r2in.at[j])

    def transpose(k0, k1):
        @pl.loop(k0, k1)
        def _(k):
            r = pl.ds(pl.multiple_of(k * 256, 256), 256)
            ft[:, r] = f[r, :].T

    def operator_first():
        for j in range(BLOCKS):
            vb[j] = d[j].astype(BF)
        for i in range(2):
            xsrc[i] = g[i]
        pl.semaphore_wait(barrier, 7 + N_MP - 1)
        ag.first(0)
        ag.first(1)
        f_loads[0].wait()
        f_loads[1].wait()
        transpose(0, 6)
        ag.second(0)
        ag.first(2)
        ag.first(3)
        ag.second(1)
        xg.first(0)
        xg.first(1)
        f_loads[2].wait()
        f_loads[3].wait()
        transpose(6, 12)
        ag.third(0)
        ag.second(2)
        ag.second(3)
        c_load.wait()
        fill(0)

        @pl.loop(0, BLOCKS)
        def _(j):
            p1(j)

            @pl.when(j < BLOCKS - 1)
            def _():
                ag.third(j + 1)

            @pl.when(j >= 1)
            def _():
                r1(j - 1, False)

            @pl.when(j == 0)
            def _():
                xg.second(0)
                xg.second(1)

            p2(j, 0, False)

            @pl.when(j >= 2)
            def _():
                r3(j - 2)

            @pl.when(j < BLOCKS - 1)
            def _():
                fill(j + 1)

            @pl.when((j >= 1) & (j < 3))
            def _():
                xg.third(j - 1)

            @pl.when(j >= 3)
            def _():
                r4(j - 3)
                xsrc[2] = w[0]
                xg.first(2)

            p2(j, 1, False)

        last = BLOCKS - 1
        r1(last, False)
        r3(last - 1)
        r4(last - 2)
        xsrc[3] = w[1]
        xg.first(3)
        r3(last)
        xg.second(2)
        r4(last - 1)
        r4(last)

    def operator_second(step, beta):
        for j in (2, 3):
            near = d[j].astype(BF)
            vb[j] = near
            lsrc[j - 2] = (d[j] - near.astype(F32)).astype(BF)
        ag.first(2)
        ag.first(3)
        lg.first(0)
        lg.first(1)
        local(0, step, beta)

        @pl.loop(0, BLOCKS)
        def _(j):
            p1(j)

            @pl.when(j == 0)
            def _():
                xg.third(3)

            @pl.when(j == 1)
            def _():
                ag.third(2)
                pd(0)

            @pl.when(j == 2)
            def _():
                pd(1)

            @pl.when(j == 3)
            def _():
                lg.third(1)
                lg.landed(0)
                pd_rest(2)

            @pl.when(j >= 1)
            def _():
                r1(j - 1, True)

            p2(j, 0, True)

            @pl.when(j == 0)
            def _():
                xg.drain(1)
                xg.landed(1)
                xg.landed(3)
                ag.second(2)
                ag.second(3)
                local(1, step, beta)

            @pl.when(j == 1)
            def _():
                ag.third(3)

            @pl.when(j == 2)
            def _():
                lg.third(0)
                fill(3)

            @pl.when(j >= 3)
            def _():
                r4_low(j - 3)

            p2(j, 1, True)

            @pl.when(j == 0)
            def _():
                lg.second(0)
                lg.second(1)

            @pl.when(j == 1)
            def _():
                fill(2)

        last = BLOCKS - 1
        lg.landed(1)
        pd_rest(3)
        dv = d[...]
        value = total(pdv[...]) / TOKENS + DAMP * total(dv * dv)
        one_row[...] = jnp.broadcast_to(value, (1, 128))

        to_group(one_row, one_tab, 1)
        r1(last, True)
        r4_low(last - 2)

        from_group(one_tab, 1)
        to_mp(1, (jnp.sum(one_tab[...], axis=0),))
        r4_low(last - 1)
        r4_low(last)

    def total(x):
        return jnp.sum(jnp.sum(jnp.sum(x, axis=0), axis=0, keepdims=True), axis=1, keepdims=True)

    def put(buf, values):
        buf[...] = jnp.zeros((8, 128), F32)
        for k, x in enumerate(values):
            buf[pl.ds(k, 1), :] = jnp.broadcast_to(x, (1, 128))

    def to_group(src, dst, i):
        @pl.loop(1, GROUP)
        def _(k):
            copy(src, dst.at[me], es.at[i], er.at[i], lax.rem(me + k, GROUP)).start()

        dst[me] = src[...]

    def from_group(dst, i):
        rest = dst.at[pl.ds(0, GROUP - 1)]
        copy(rest, rest, es.at[i], er.at[i], partner).wait()

    def over_mp(src, dst, i, k):
        return pltpu.make_async_remote_copy(
            src_ref=src, dst_ref=dst, send_sem=es.at[i], recv_sem=er.at[i],
            device_id={"mp": lax.rem(mx + k, N_MP)}, device_id_type=MESH,
        )

    def to_mp(turn, values):
        put(row2.at[turn], values)
        for k in range(1, N_MP):
            over_mp(row2.at[turn], tab2.at[turn, mx], 2 + turn, k).start()
        tab2[turn, mx] = row2[turn]

    def from_mp(turn):
        rest = tab2.at[turn, pl.ds(0, N_MP - 1)]
        over_mp(rest, rest, 2 + turn, 1).wait()
        return tab2[turn]

    def column(tb, k):
        return tb[:, k : k + 1, :]

    def moved(tb, x):
        ww, uu, uw, at = (column(tb, k) for k in (2, 3, 4, 5))
        gap = at - x
        return jnp.sum(uu + gap * (2.0 * uw + gap * ww), axis=0), jnp.sum(uw + gap * ww, axis=0)

    def ratio(p, q):
        return jnp.where(q > 0, p / jnp.where(q > 0, q, 1.0), 0.0)

    def centre(tb):
        gg, gw, ww = (jnp.sum(column(tb, k), axis=0) for k in range(3))
        x = ratio(gw, ww)
        uu, uw = moved(tb, x)
        return gg, gw, ww, uu, uw, x

    pltpu.make_async_copy(g, g, ld.at[0]).wait()
    d[...] = g[...]
    operator_first()
    gv, wv = g[...], w[...]
    gg, gw, ww = total(gv * gv), total(gv * wv), total(wv * wv)
    x = ratio(gw, ww)
    u = gv - x * wv
    for j in range(BLOCKS):
        ag.drain(j)
    put(row, (gg, gw, ww, total(u * u), total(u * wv), x))
    to_group(row, tab, 0)
    xg.second(3)
    xg.third(2)
    drain(False)
    from_group(tab, 0)
    to_mp(0, centre(tab[...]))
    xg.drain(0)
    xg.landed(0)
    xg.landed(2)
    tb = from_mp(0)
    norm = jnp.sum(column(tb, 0), axis=0)
    step = norm / jnp.sum(column(tb, 1), axis=0)
    norm_next, _ = moved(tb, step)
    beta = (norm_next / norm)[:, :1]
    step = step[:, :1]
    sol[...] = step * gv
    res = gv - step * wv
    g[...] = res
    d[...] = res + beta * gv
    operator_second(step, beta)
    tb = from_mp(1)
    step = (norm_next / jnp.sum(column(tb, 0), axis=0))[:, :1]
    dv, wv = d[...], w[...]
    for j in range(BLOCKS):
        cols = pl.ds(j * NB, NB)
        sol_o[:, cols] = sol[j] + step * dv[j]
        res_o[:, cols] = g[j] - step * wv[j]
    drain(True)
    for j in (2, 3):
        ag.drain(j)
        xg.drain(j)
        lg.drain(j - 2)


def shards(features, curvature, task_grad):
    any_spec = pl.BlockSpec(memory_space=pltpu.HBM)
    out = jax.ShapeDtypeStruct(task_grad.shape, F32)
    small = (BLOCKS, ROWS, NB)
    return pl.pallas_call(
        kernel,
        out_shape=(out, out),
        in_specs=[any_spec] * 3,
        out_specs=(pl.BlockSpec(memory_space=pltpu.VMEM),) * 2,
        scratch_shapes=[
            pltpu.VMEM((TOK, DIN), BF),
            pltpu.VMEM((DIN, TOK), BF),
            pltpu.VMEM((TOK, COLS), BF),
            pltpu.VMEM(small, F32),
            pltpu.VMEM(small, F32),
            pltpu.VMEM(small, F32),
            pltpu.VMEM(small, F32),
            pltpu.VMEM(small, BF),
            pltpu.VMEM((BLOCKS, 16, ROWS, NB), BF),
            pltpu.VMEM((BLOCKS, 16, ROWS, NB), BF),
            pltpu.VMEM((BLOCKS, RING, RING, 2, ROWS, NB), BF),
            pltpu.VMEM((TOK, NB), BF),
            pltpu.VMEM((BLOCKS, RING, RING, 2, ROWS, NB), F32),
            pltpu.VMEM((BLOCKS, RING, RING, 2, ROWS, NB), BF),
            pltpu.VMEM((BLOCKS, RING, RING, ROWS, NB), F32),
            pltpu.VMEM((BLOCKS, RING, RING, ROWS, NB), BF),
            pltpu.VMEM((BLOCKS, 16, ROWS, NB), F32),
            pltpu.VMEM((BLOCKS, 16, ROWS, NB), BF),
            pltpu.VMEM((BLOCKS, 3, RING, ROWS, NB), F32),
            pltpu.VMEM((BLOCKS, RING, ROWS, NB), F32),
            pltpu.VMEM((BLOCKS, 3, ROWS, NB), F32),
            pltpu.VMEM((BLOCKS, 16, ROWS, NB), BF),
            pltpu.VMEM((4, ROWS, NB), F32),
            pltpu.VMEM((4, 16, ROWS, NB), F32),
            pltpu.VMEM((4, 16, ROWS, NB), F32),
            pltpu.VMEM((2, ROWS, NB), BF),
            pltpu.VMEM((2, 16, ROWS, NB), BF),
            pltpu.VMEM((2, 16, ROWS, NB), BF),
            pltpu.VMEM(small, F32),
            pltpu.VMEM((8, 128), F32),
            pltpu.VMEM((GROUP, 8, 128), F32),
            pltpu.VMEM((1, 128), F32),
            pltpu.VMEM((GROUP, 1, 128), F32),
            pltpu.VMEM((2, 8, 128), F32),
            pltpu.VMEM((2, N_MP, 8, 128), F32),
            pltpu.SemaphoreType.DMA((BLOCKS + 6, 3)),
            pltpu.SemaphoreType.DMA((BLOCKS + 6, 3)),
            pltpu.SemaphoreType.DMA((BLOCKS, 4)),
            pltpu.SemaphoreType.DMA((BLOCKS, 4)),
            pltpu.SemaphoreType.DMA((4,)),
            pltpu.SemaphoreType.DMA((4,)),
            pltpu.SemaphoreType.DMA((6,)),
        ],
        compiler_params=pltpu.CompilerParams(
            collective_id=0, has_side_effects=True, vmem_limit_bytes=51 * 2**20
        ),
    )(features, curvature, pltpu.with_memory_space_constraint(task_grad, pltpu.HBM))


def solution(mesh):
    placed = (P("dp", None), P("dp", "mp"), P("dp", "mp"))
    return jax.shard_map(
        shards,
        mesh=mesh,
        in_specs=placed,
        out_specs=(P("dp", "mp"), P("dp", "mp")),
        check_vma=False,
    )
```

```python
import functools

import jax
import jax.numpy as jnp
from jax import lax
from jax.experimental import pallas as pl
from jax.experimental.pallas import tpu as pltpu
from jax.sharding import PartitionSpec as P

RING = 4
GROUP = 32
N_MP = 4
TOK = 3072
DIN = 1024
COLS = 1024
NB = 256
BLOCKS = COLS // NB
ROWS = DIN // GROUP
TOKENS = 98304.0
DAMP = 0.5
MESH = pl.DeviceIdType.MESH
BF, F32 = jnp.bfloat16, jnp.float32
FAR_FIRST = sorted(
    ((i, k) for i in range(RING) for k in range(RING) if i or k),
    key=lambda t: -min(t[0], RING - t[0]) - min(t[1], RING - t[1]),
)


def kernel(
    f_h, c_h, g_h, sol_o, res_o,
    f, ft, cv, g, d, w, sol, vb, g_own, g_par, v, wt,
    acc, accb, d0, d0b, s, sb, rin, t, r2in,
    din, xsrc, xo, xp, lsrc, lo, lp, pdv, row, tab, one_row, one_tab,
    gs, gr, qs, qr, es, er, ld,
):
    me = lax.axis_index("dp")
    mx = lax.axis_index("mp")
    c = lax.rem(me, 2)
    chip = me // 2
    z = chip // RING
    y = lax.rem(chip, RING)
    pa = (1 - c) * y + c * z
    pb = (1 - c) * z + c * y

    def a_at(k):
        q = lax.rem(pa + k, RING)
        return ((1 - c) * (z * RING + q) + c * (q * RING + y)) * 2 + c

    def b_at(k):
        q = lax.rem(pb + k, RING)
        return ((1 - c) * (q * RING + y) + c * (z * RING + q)) * 2 + c

    partner = me + 1 - 2 * c
    a_up, a_dn, a_op = a_at(1), a_at(3), a_at(2)
    b_up, b_dn, b_op = b_at(1), b_at(3), b_at(2)
    qa_up, qa_dn, qa_op = lax.rem(pa + 1, RING), lax.rem(pa + 3, RING), lax.rem(pa + 2, RING)
    qb_up, qb_dn, qb_op = lax.rem(pb + 1, RING), lax.rem(pb + 3, RING), lax.rem(pb + 2, RING)

    loads = [
        pltpu.make_async_copy(g_h.at[:, pl.ds(j * NB, NB)], g.at[j], ld.at[0])
        for j in range(BLOCKS)
    ]
    parts = 4
    f_loads = [
        pltpu.make_async_copy(
            f_h.at[pl.ds(k * (TOK // parts), TOK // parts)],
            f.at[pl.ds(k * (TOK // parts), TOK // parts)],
            ld.at[1 + k],
        )
        for k in range(parts)
    ]
    c_load = pltpu.make_async_copy(c_h, cv, ld.at[1 + parts])
    for x in (*loads, *f_loads, c_load):
        x.start()

    barrier = pltpu.get_barrier_semaphore()

    for q in (a_up, a_dn, a_op, b_up, b_dn, b_op, partner):
        pl.semaphore_signal(barrier, inc=1, device_id={"dp": q}, device_id_type=MESH)

    for k in range(1, N_MP):
        pl.semaphore_signal(
            barrier, inc=1, device_id={"mp": lax.rem(mx + k, N_MP)}, device_id_type=MESH
        )

    def copy(src, dst, sends, recvs, dev):
        return pltpu.make_async_remote_copy(
            src_ref=src, dst_ref=dst, send_sem=sends, recv_sem=recvs,
            device_id={"dp": dev}, device_id_type=MESH,
        )

    def send(j, i, src, dst, dev):
        copy(src, dst, qs.at[j, i], qr.at[j, i], dev).start()

    def got(j, i, whole):
        copy(whole, whole, qs.at[j, i], qr.at[j, i], partner).wait_recv()

    def sent(j, i, whole):
        copy(whole, whole, qs.at[j, i], qr.at[j, i], partner).wait_send()

    def strip(buf, j, q):
        return buf.at[j, pl.ds(q * RING, RING)]

    class Gather:
        def __init__(self, src, own, par, base):
            self.src, self.own, self.par, self.base = src, own, par, base

        def copy(self, j, i, src, dst, dev):
            return copy(src, dst, gs.at[self.base + j, i], gr.at[self.base + j, i], dev)

        def got(self, j, i, pieces):
            part = self.own.at[j, pl.ds(0, pieces)]
            self.copy(j, i, part, part, partner).wait_recv()

        def first(self, j):
            at = pb * RING + pa
            for dev in (a_up, a_dn, a_op):
                self.copy(j, 0, self.src.at[j], self.own.at[j, at], dev).start()
            self.own[j, at] = self.src[j]

        def second(self, j):
            self.got(j, 0, 3)
            mine = strip(self.own, j, pb)
            for dev in (b_up, b_dn, b_op):
                self.copy(j, 1, mine, mine, dev).start()
            self.copy(j, 2, mine, strip(self.par, j, pb), partner).start()

        def third(self, j):
            self.got(j, 1, 12)
            for q in (qb_dn, qb_up, qb_op):
                self.copy(j, 2, strip(self.own, j, q), strip(self.par, j, q), partner).start()

        def landed(self, j):
            self.got(j, 2, 16)

        def drain(self, j):
            for i, pieces in enumerate((3, 12, 16)):
                part = self.own.at[j, pl.ds(0, pieces)]
                self.copy(j, i, part, part, partner).wait_send()

    ag = Gather(vb, g_own, g_par, 0)
    xg = Gather(xsrc, xo, xp, BLOCKS)
    lg = Gather(lsrc, lo, lp, 0)

    def places():
        for zz in range(RING):
            for yy in range(RING):
                zy, yz = zz * RING + yy, yy * RING + zz
                yield zz, yy, (1 - c) * zy + c * yz, (1 - c) * yz + c * zy

    def fill(j):
        ag.landed(j)
        for zz, yy, mine, other in places():
            v[j, zz, yy, c] = g_own[j, mine]
            v[j, zz, yy, 1 - c] = g_par[j, other]

    def local(j, step, beta):
        for zz, yy, mine, other in places():
            for buf, at, core in ((xo, mine, c), (xp, other, 1 - c)):
                gv = buf[j, at]
                nxt = (gv - step * buf[2 + j, at]) + beta * gv
                buf[j, at] = nxt
                v[j, zz, yy, core] = nxt.astype(BF)

    def pd(j):
        part = jnp.zeros((ROWS, NB), F32)
        for zz, yy, mine, other in places():
            part += acc[j, zz, yy, c] * xo[j, mine] + acc[j, zz, yy, 1 - c] * xp[j, other]
        pdv[j] = part

    def pd_rest(j):
        part = jnp.zeros((ROWS, NB), F32)
        for zz, yy, mine, other in places():
            for core, rest in ((c, lo[j - 2, mine]), (1 - c, lp[j - 2, other])):
                part += acc[j, zz, yy, core] * (v[j, zz, yy, core].astype(F32) + rest.astype(F32))
        pdv[j] = part

    def alone(j):
        return pl.loop(0, (j + BLOCKS) // BLOCKS)

    def p1(j):
        cols = pl.ds(pl.multiple_of(j * NB, NB), NB)

        @alone(j)
        def _(_):
            p = jnp.dot(f[...], v[j].reshape(DIN, NB), preferred_element_type=F32)
            wt[...] = (cv[:, cols].astype(F32) * p).astype(BF)

    def p2(j, z0, zn, low):
        r = pl.ds(z0 * (DIN // RING), zn * (DIN // RING))
        zs = pl.ds(z0, zn)

        @alone(j)
        def _(_):
            out = jnp.dot(ft[r, :], wt[...], preferred_element_type=F32)
            out = out.reshape(zn, RING, 2, ROWS, NB)
            acc[j, zs] = out
            if low:
                accb[j, zs] = out.astype(BF)

        src, dst = (accb, d0b) if low else (acc, d0)
        send(j, 0, src.at[j, zs, :, 1 - c], dst.at[j, zs], partner)

    def p2_start(j, low):
        halves = j % 2 == 1 if low else j == BLOCKS - 1

        @pl.when(~halves)
        def _():
            p2(j, 0, RING, low)

        @pl.when(halves)
        def _():
            p2(j, 0, RING // 2, low)

    def p2_end(j, low):
        @pl.when(j % 2 == 1 if low else j == BLOCKS - 1)
        def _():
            p2(j, RING // 2, RING // 2, low)

    def r1(j, low):
        src = d0b if low else d0
        got(j, 0, src.at[j])
        for zz, yy, _, at in places():
            both = acc[j, zz, yy, c] + src[j, zz, yy].astype(F32)
            s[j, at] = both
            if low:
                sb[j, at] = both.astype(BF)
        if low:
            for ka, kb in FAR_FIRST:
                piece(j, ka, kb)
        else:
            send(j, 1, strip(s, j, qa_up), rin.at[j, 0], a_up)
            send(j, 1, strip(s, j, qa_dn), rin.at[j, 1], a_dn)
            send(j, 1, strip(s, j, qa_op), rin.at[j, 2], a_op)

    def piece(j, ka, kb):
        qa, qb = lax.rem(pa + ka, RING), lax.rem(pb + kb, RING)
        dev = ((1 - c) * (qb * RING + qa) + c * (qa * RING + qb)) * 2 + c
        send(j, 1, sb.at[j, qa * RING + qb], din.at[j, ka * RING + kb], dev)

    def r4_low(j):
        got(j, 1, din.at[j, pl.ds(1, 15)])
        total = s[j, pa * RING + pb]
        for k in range(1, 16):
            total += din[j, k].astype(F32)
        w[j] = total / TOKENS + DAMP * d[j]

    def r3(j):
        got(j, 1, rin.at[j])
        mine = s[j, pl.ds(pa * RING, RING)]
        t[j] = (mine + rin[j, 2]) + (rin[j, 0] + rin[j, 1])
        send(j, 2, t.at[j, qb_up], r2in.at[j, 0], b_up)
        send(j, 2, t.at[j, qb_dn], r2in.at[j, 1], b_dn)
        send(j, 2, t.at[j, qb_op], r2in.at[j, 2], b_op)

    def r4(j):
        got(j, 2, r2in.at[j])
        total = (t[j, pb] + r2in[j, 2]) + (r2in[j, 0] + r2in[j, 1])
        w[j] = total / TOKENS + DAMP * d[j]

    def drain(low):
        for j in range(BLOCKS):
            sent(j, 0, (d0b if low else d0).at[j])
            if low:
                sent(j, 1, din.at[j, pl.ds(1, 15)])
            else:
                sent(j, 1, rin.at[j])
                sent(j, 2, r2in.at[j])

    def transpose(k0, k1):
        @pl.loop(k0, k1)
        def _(k):
            r = pl.ds(pl.multiple_of(k * 256, 256), 256)
            ft[:, r] = f[r, :].T

    def operator_first():
        for j in range(BLOCKS):
            vb[j] = d[j].astype(BF)
        for i in range(2):
            xsrc[i] = g[i]
        pl.semaphore_wait(barrier, 7 + N_MP - 1)
        ag.first(0)
        ag.first(1)
        f_loads[0].wait()
        f_loads[1].wait()
        transpose(0, 6)
        ag.second(0)
        ag.first(2)
        ag.first(3)
        ag.second(1)
        xg.first(0)
        xg.first(1)
        f_loads[2].wait()
        f_loads[3].wait()
        transpose(6, 12)
        ag.third(0)
        ag.second(2)
        ag.second(3)
        c_load.wait()
        fill(0)

        @pl.loop(0, BLOCKS)
        def _(j):
            p1(j)

            @pl.when(j < BLOCKS - 1)
            def _():
                ag.third(j + 1)

            @pl.when(j >= 1)
            def _():
                r1(j - 1, False)

            @pl.when(j == 0)
            def _():
                xg.second(0)
                xg.second(1)

            @pl.when(j == 3)
            def _():
                r3(0)

            p2_start(j, False)

            @pl.when(j == 3)
            def _():
                r3(1)

            @pl.when(j < BLOCKS - 1)
            def _():
                fill(j + 1)

            @pl.when((j >= 1) & (j < 3))
            def _():
                xg.third(j - 1)

            p2_end(j, False)

        last = BLOCKS - 1
        r1(last, False)
        r4(last - 3)
        xsrc[2] = w[0]
        xg.first(2)
        r3(last - 1)
        r4(last - 2)
        xsrc[3] = w[1]
        xg.first(3)
        r3(last)
        xg.second(2)
        r4(last - 1)
        r4(last)

    def operator_second(step, beta):
        for j in (2, 3):
            near = d[j].astype(BF)
            vb[j] = near
            lsrc[j - 2] = (d[j] - near.astype(F32)).astype(BF)
        ag.first(2)
        ag.first(3)
        lg.first(0)
        lg.first(1)
        local(0, step, beta)

        @pl.loop(0, BLOCKS)
        def _(j):
            p1(j)

            @pl.when(j == 0)
            def _():
                xg.third(3)

            @pl.when(j == 1)
            def _():
                pd(0)

            @pl.when(j == 2)
            def _():
                pd(1)

            @pl.when(j == 3)
            def _():
                lg.third(1)
                lg.landed(0)
                pd_rest(2)

            @pl.when(j >= 1)
            def _():
                r1(j - 1, True)

            p2_start(j, True)

            @pl.when(j == 0)
            def _():
                xg.drain(1)
                xg.landed(1)
                xg.landed(3)
                ag.second(2)
                ag.second(3)
                local(1, step, beta)

            @pl.when(j == 1)
            def _():
                ag.third(2)
                ag.third(3)

            @pl.when(j == 2)
            def _():
                lg.third(0)
                fill(3)

            @pl.when(j >= 3)
            def _():
                r4_low(j - 3)

            p2_end(j, True)

            @pl.when(j == 0)
            def _():
                lg.second(0)
                lg.second(1)

            @pl.when(j == 1)
            def _():
                fill(2)

        last = BLOCKS - 1
        lg.landed(1)
        pd_rest(3)
        dv = d[...]
        value = total(pdv[...]) / TOKENS + DAMP * total(dv * dv)
        one_row[...] = jnp.broadcast_to(value, (1, 128))

        to_far(one_row, one_tab, 1)
        r1(last, True)
        to_near(one_row, one_tab, 1)
        r4_low(last - 2)

        r4_low(last - 1)
        r4_low(last)
        from_all(one_tab, 1)

    def total(x):
        return jnp.sum(jnp.sum(jnp.sum(x, axis=0), axis=0, keepdims=True), axis=1, keepdims=True)

    def to_device(src, dst, i, dp, mp):
        pltpu.make_async_remote_copy(
            src_ref=src, dst_ref=dst.at[mx * GROUP + me], send_sem=es.at[i], recv_sem=er.at[i],
            device_id={"dp": dp, "mp": mp}, device_id_type=MESH,
        ).start()

    def to_group(src, dst, i, k):
        mp = lax.rem(mx + k, N_MP)

        @pl.loop(0, GROUP, unroll=8)
        def _(q):
            to_device(src, dst, i, lax.rem(me + q + GROUP // 2 + 2, GROUP), mp)

    def to_far(src, dst, i):
        to_group(src, dst, i, 2)
        to_group(src, dst, i, 1)

    def to_near(src, dst, i):
        to_group(src, dst, i, 3)

        @pl.loop(1, GROUP)
        def _(q):
            to_device(src, dst, i, lax.rem(me + q, GROUP), mx)

        dst[mx * GROUP + me] = src[...]

    def from_all(dst, i):
        rest = dst.at[pl.ds(0, GROUP * N_MP - 1)]
        copy(rest, rest, es.at[i], er.at[i], partner).wait()

    lane = lax.broadcasted_iota(jnp.int32, (1, 128), 1)

    def at_lane(x, k):
        return jnp.sum(jnp.where(lane == k, x, 0.0), axis=1, keepdims=True)

    def scalars(tb):
        sums, x = tb[:, 0:1, :], tb[:, 1:2, :]
        all_sums = jnp.sum(sums, axis=0)
        norm = at_lane(all_sums, 3)
        step = norm / at_lane(all_sums, 4)
        gap = x - step[None]
        at = lane[None]
        factor = jnp.where(at == 0, 1.0, jnp.where(at == 1, gap, jnp.where(at == 2, gap * gap, 0.0)))
        return norm, step, jnp.sum(jnp.sum(sums * factor, axis=0), axis=1, keepdims=True)

    def ratio(p, q):
        return jnp.where(q > 0, p / jnp.where(q > 0, q, 1.0), 0.0)

    pltpu.make_async_copy(g, g, ld.at[0]).wait()
    d[...] = g[...]
    operator_first()
    gv, wv = g[...], w[...]
    gg, gw, ww = total(gv * gv), total(gv * wv), total(wv * wv)
    x = ratio(gw, ww)
    u = gv - x * wv
    for j in range(BLOCKS):
        ag.drain(j)
    packed = jnp.zeros((1, 128), F32)
    for k, value in enumerate((total(u * u), 2.0 * total(u * wv), ww, gg, gw)):
        packed = jnp.where(lane == k, value, packed)
    row[0:1, :] = packed
    row[1:2, :] = jnp.broadcast_to(x, (1, 128))
    to_far(row, tab, 0)
    to_near(row, tab, 0)
    xg.second(3)
    xg.third(2)
    drain(False)
    xg.drain(0)
    xg.landed(0)
    xg.landed(2)
    from_all(tab, 0)
    norm, step, norm_next = scalars(tab[...])
    beta = norm_next / norm
    sol[...] = step * gv
    res = gv - step * wv
    g[...] = res
    d[...] = res + beta * gv
    operator_second(step, beta)
    step = norm_next / jnp.sum(one_tab[...], axis=0)[:, :1]
    dv, wv = d[...], w[...]
    for j in range(BLOCKS):
        cols = pl.ds(j * NB, NB)
        sol_o[:, cols] = sol[j] + step * dv[j]
        res_o[:, cols] = g[j] - step * wv[j]
    drain(True)
    for j in (2, 3):
        ag.drain(j)
        xg.drain(j)
        lg.drain(j - 2)


def shards(features, curvature, task_grad):
    any_spec = pl.BlockSpec(memory_space=pltpu.HBM)
    out = jax.ShapeDtypeStruct(task_grad.shape, F32)
    small = (BLOCKS, ROWS, NB)
    return pl.pallas_call(
        kernel,
        out_shape=(out, out),
        in_specs=[any_spec] * 3,
        out_specs=(pl.BlockSpec(memory_space=pltpu.VMEM),) * 2,
        scratch_shapes=[
            pltpu.VMEM((TOK, DIN), BF),
            pltpu.VMEM((DIN, TOK), BF),
            pltpu.VMEM((TOK, COLS), BF),
            pltpu.VMEM(small, F32),
            pltpu.VMEM(small, F32),
            pltpu.VMEM(small, F32),
            pltpu.VMEM(small, F32),
            pltpu.VMEM(small, BF),
            pltpu.VMEM((BLOCKS, 16, ROWS, NB), BF),
            pltpu.VMEM((BLOCKS, 16, ROWS, NB), BF),
            pltpu.VMEM((BLOCKS, RING, RING, 2, ROWS, NB), BF),
            pltpu.VMEM((TOK, NB), BF),
            pltpu.VMEM((BLOCKS, RING, RING, 2, ROWS, NB), F32),
            pltpu.VMEM((BLOCKS, RING, RING, 2, ROWS, NB), BF),
            pltpu.VMEM((BLOCKS, RING, RING, ROWS, NB), F32),
            pltpu.VMEM((BLOCKS, RING, RING, ROWS, NB), BF),
            pltpu.VMEM((BLOCKS, 16, ROWS, NB), F32),
            pltpu.VMEM((BLOCKS, 16, ROWS, NB), BF),
            pltpu.VMEM((BLOCKS, 3, RING, ROWS, NB), F32),
            pltpu.VMEM((BLOCKS, RING, ROWS, NB), F32),
            pltpu.VMEM((BLOCKS, 3, ROWS, NB), F32),
            pltpu.VMEM((BLOCKS, 16, ROWS, NB), BF),
            pltpu.VMEM((4, ROWS, NB), F32),
            pltpu.VMEM((4, 16, ROWS, NB), F32),
            pltpu.VMEM((4, 16, ROWS, NB), F32),
            pltpu.VMEM((2, ROWS, NB), BF),
            pltpu.VMEM((2, 16, ROWS, NB), BF),
            pltpu.VMEM((2, 16, ROWS, NB), BF),
            pltpu.VMEM(small, F32),
            pltpu.VMEM((2, 128), F32),
            pltpu.VMEM((GROUP * N_MP, 2, 128), F32),
            pltpu.VMEM((1, 128), F32),
            pltpu.VMEM((GROUP * N_MP, 1, 128), F32),
            pltpu.SemaphoreType.DMA((BLOCKS + 4, 3)),
            pltpu.SemaphoreType.DMA((BLOCKS + 4, 3)),
            pltpu.SemaphoreType.DMA((BLOCKS, 3)),
            pltpu.SemaphoreType.DMA((BLOCKS, 3)),
            pltpu.SemaphoreType.DMA((2,)),
            pltpu.SemaphoreType.DMA((2,)),
            pltpu.SemaphoreType.DMA((6,)),
        ],
        compiler_params=pltpu.CompilerParams(
            collective_id=0, has_side_effects=True, vmem_limit_bytes=51 * 2**20
        ),
    )(features, curvature, pltpu.with_memory_space_constraint(task_grad, pltpu.HBM))


def solution(mesh):
    placed = (P("dp", None), P("dp", "mp"), P("dp", "mp"))
    return jax.shard_map(
        shards,
        mesh=mesh,
        in_specs=placed,
        out_specs=(P("dp", "mp"), P("dp", "mp")),
        check_vma=False,
    )
```

```python
import functools

import jax
import jax.numpy as jnp
from jax import lax
from jax.experimental import pallas as pl
from jax.experimental.pallas import tpu as pltpu
from jax.sharding import PartitionSpec as P

RING = 4
GROUP = 32
N_MP = 4
TOK = 3072
DIN = 1024
COLS = 1024
NB = 256
BLOCKS = COLS // NB
ROWS = DIN // GROUP
TOKENS = 98304.0
DAMP = 0.5
MESH = pl.DeviceIdType.MESH
BF, F32 = jnp.bfloat16, jnp.float32
FAR_FIRST = sorted(
    ((i, k) for i in range(RING) for k in range(RING) if i or k),
    key=lambda t: -min(t[0], RING - t[0]) - min(t[1], RING - t[1]),
)


def kernel(
    f_h, c_h, g_h, sol_o, res_o,
    f, ft, cv, g, d, w, sol, vb, g_own, g_par, v, wt,
    acc, accb, d0, d0b, s, sb, rin, t, r2in,
    din, xsrc, xo, xp, lsrc, lo, lp, pdv, row, tab, one_row, one_tab,
    gs, gr, qs, qr, es, er, ld,
):
    me = lax.axis_index("dp")
    mx = lax.axis_index("mp")
    c = lax.rem(me, 2)
    chip = me // 2
    z = chip // RING
    y = lax.rem(chip, RING)
    pa = (1 - c) * y + c * z
    pb = (1 - c) * z + c * y

    def a_at(k):
        q = lax.rem(pa + k, RING)
        return ((1 - c) * (z * RING + q) + c * (q * RING + y)) * 2 + c

    def b_at(k):
        q = lax.rem(pb + k, RING)
        return ((1 - c) * (q * RING + y) + c * (z * RING + q)) * 2 + c

    partner = me + 1 - 2 * c
    a_up, a_dn, a_op = a_at(1), a_at(3), a_at(2)
    b_up, b_dn, b_op = b_at(1), b_at(3), b_at(2)
    qa_up, qa_dn, qa_op = lax.rem(pa + 1, RING), lax.rem(pa + 3, RING), lax.rem(pa + 2, RING)
    qb_up, qb_dn, qb_op = lax.rem(pb + 1, RING), lax.rem(pb + 3, RING), lax.rem(pb + 2, RING)

    loads = [
        pltpu.make_async_copy(g_h.at[:, pl.ds(j * NB, NB)], g.at[j], ld.at[0])
        for j in range(BLOCKS)
    ]
    parts = 4
    f_loads = [
        pltpu.make_async_copy(
            f_h.at[pl.ds(k * (TOK // parts), TOK // parts)],
            f.at[pl.ds(k * (TOK // parts), TOK // parts)],
            ld.at[1 + k],
        )
        for k in range(parts)
    ]
    c_load = pltpu.make_async_copy(c_h, cv, ld.at[1 + parts])
    for x in (*loads, *f_loads, c_load):
        x.start()

    barrier = pltpu.get_barrier_semaphore()

    for q in (a_up, a_dn, a_op, b_up, b_dn, b_op, partner):
        pl.semaphore_signal(barrier, inc=1, device_id={"dp": q}, device_id_type=MESH)

    for k in range(1, N_MP):
        pl.semaphore_signal(
            barrier, inc=1, device_id={"mp": lax.rem(mx + k, N_MP)}, device_id_type=MESH
        )

    def copy(src, dst, sends, recvs, dev):
        return pltpu.make_async_remote_copy(
            src_ref=src, dst_ref=dst, send_sem=sends, recv_sem=recvs,
            device_id={"dp": dev}, device_id_type=MESH,
        )

    def send(j, i, src, dst, dev):
        copy(src, dst, qs.at[j, i], qr.at[j, i], dev).start()

    def got(j, i, whole):
        copy(whole, whole, qs.at[j, i], qr.at[j, i], partner).wait_recv()

    def sent(j, i, whole):
        copy(whole, whole, qs.at[j, i], qr.at[j, i], partner).wait_send()

    def strip(buf, j, q):
        return buf.at[j, pl.ds(q * RING, RING)]

    class Gather:
        def __init__(self, src, own, par, base):
            self.src, self.own, self.par, self.base = src, own, par, base

        def copy(self, j, i, src, dst, dev):
            return copy(src, dst, gs.at[self.base + j, i], gr.at[self.base + j, i], dev)

        def got(self, j, i, pieces):
            part = self.own.at[j, pl.ds(0, pieces)]
            self.copy(j, i, part, part, partner).wait_recv()

        def first(self, j):
            at = pb * RING + pa
            for dev in (a_up, a_dn, a_op):
                self.copy(j, 0, self.src.at[j], self.own.at[j, at], dev).start()
            self.own[j, at] = self.src[j]

        def second(self, j):
            self.got(j, 0, 3)
            mine = strip(self.own, j, pb)
            for dev in (b_up, b_dn, b_op):
                self.copy(j, 1, mine, mine, dev).start()
            self.copy(j, 2, mine, strip(self.par, j, pb), partner).start()

        def third(self, j):
            self.got(j, 1, 12)
            for q in (qb_dn, qb_up, qb_op):
                self.copy(j, 2, strip(self.own, j, q), strip(self.par, j, q), partner).start()

        def landed(self, j):
            self.got(j, 2, 16)

        def drain(self, j):
            for i, pieces in enumerate((3, 12, 16)):
                part = self.own.at[j, pl.ds(0, pieces)]
                self.copy(j, i, part, part, partner).wait_send()

    ag = Gather(vb, g_own, g_par, 0)
    xg = Gather(xsrc, xo, xp, BLOCKS)
    lg = Gather(lsrc, lo, lp, 0)

    def places():
        for zz in range(RING):
            for yy in range(RING):
                zy, yz = zz * RING + yy, yy * RING + zz
                yield zz, yy, (1 - c) * zy + c * yz, (1 - c) * yz + c * zy

    def fill(j):
        ag.landed(j)
        for zz, yy, mine, other in places():
            v[j, zz, yy, c] = g_own[j, mine]
            v[j, zz, yy, 1 - c] = g_par[j, other]

    def local(j, step, beta):
        for zz, yy, mine, other in places():
            for buf, at, core in ((xo, mine, c), (xp, other, 1 - c)):
                gv = buf[j, at]
                nxt = (gv - step * buf[2 + j, at]) + beta * gv
                buf[j, at] = nxt
                v[j, zz, yy, core] = nxt.astype(BF)

    def pd(j):
        part = jnp.zeros((ROWS, NB), F32)
        for zz, yy, mine, other in places():
            part += acc[j, zz, yy, c] * xo[j, mine] + acc[j, zz, yy, 1 - c] * xp[j, other]
        pdv[j] = part

    def pd_rest(j):
        part = jnp.zeros((ROWS, NB), F32)
        for zz, yy, mine, other in places():
            for core, rest in ((c, lo[j - 2, mine]), (1 - c, lp[j - 2, other])):
                part += acc[j, zz, yy, core] * (v[j, zz, yy, core].astype(F32) + rest.astype(F32))
        pdv[j] = part

    def alone(j):
        return pl.loop(0, (j + BLOCKS) // BLOCKS)

    def p1(j):
        cols = pl.ds(pl.multiple_of(j * NB, NB), NB)

        @alone(j)
        def _(_):
            p = jnp.dot(f[...], v[j].reshape(DIN, NB), preferred_element_type=F32)
            wt[...] = (cv[:, cols].astype(F32) * p).astype(BF)

    def p2(j, z0, zn, low, i=0):
        r = pl.ds(z0 * (DIN // RING), zn * (DIN // RING))
        zs = pl.ds(z0, zn)

        @alone(j)
        def _(_):
            out = jnp.dot(ft[r, :], wt[...], preferred_element_type=F32)
            out = out.reshape(zn, RING, 2, ROWS, NB)
            acc[j, zs] = out
            if low:
                accb[j, zs] = out.astype(BF)

        src, dst = (accb, d0b) if low else (acc, d0)
        send(j, i, src.at[j, zs, :, 1 - c], dst.at[j, zs], partner)

    def p2_start(j, low):
        halves = j % 2 == 1 if low else j == BLOCKS - 1

        @pl.when(~halves)
        def _():
            p2(j, 0, RING, low)

        @pl.when(halves)
        def _():
            p2(j, 0, RING // 2, low)

    def p2_end(j, low):
        @pl.when(j % 2 == 1 if low else j == BLOCKS - 1)
        def _():
            p2(j, RING // 2, RING // 2, low, 2 * (j // (BLOCKS - 1)) if low else 0)

    def r1(j, low):
        src = d0b if low else d0
        got(j, 0, src.at[j])
        for zz, yy, _, at in places():
            both = acc[j, zz, yy, c] + src[j, zz, yy].astype(F32)
            s[j, at] = both
            if low:
                sb[j, at] = both.astype(BF)
        if low:
            for ka, kb in FAR_FIRST:
                piece(j, ka, kb)
        else:
            send(j, 1, strip(s, j, qa_up), rin.at[j, 0], a_up)
            send(j, 1, strip(s, j, qa_dn), rin.at[j, 1], a_dn)
            send(j, 1, strip(s, j, qa_op), rin.at[j, 2], a_op)

    def r1_half(j, h):
        got(j, 2 * h, d0b.at[j, pl.ds(2 * h, 2)])
        for zz, yy, _, at in places():
            if zz // 2 == h:
                both = acc[j, zz, yy, c] + d0b[j, zz, yy].astype(F32)
                s[j, at] = both
                sb[j, at] = both.astype(BF)
        for zz, yy, _, at in places():
            if zz // 2 == h:

                @pl.when((zz != z) | (yy != y))
                def _(zz=zz, yy=yy, at=at):
                    ka = lax.rem((1 - c) * yy + c * zz + RING - pa, RING)
                    kb = lax.rem((1 - c) * zz + c * yy + RING - pb, RING)
                    send(j, 1, sb.at[j, at], din.at[j, ka * RING + kb], (zz * RING + yy) * 2 + c)

    def piece(j, ka, kb):
        qa, qb = lax.rem(pa + ka, RING), lax.rem(pb + kb, RING)
        dev = ((1 - c) * (qb * RING + qa) + c * (qa * RING + qb)) * 2 + c
        send(j, 1, sb.at[j, qa * RING + qb], din.at[j, ka * RING + kb], dev)

    def r4_low(j):
        got(j, 1, din.at[j, pl.ds(1, 15)])
        total = s[j, pa * RING + pb]
        for k in range(1, 16):
            total += din[j, k].astype(F32)
        w[j] = total / TOKENS + DAMP * d[j]

    def r3(j):
        got(j, 1, rin.at[j])
        mine = s[j, pl.ds(pa * RING, RING)]
        t[j] = (mine + rin[j, 2]) + (rin[j, 0] + rin[j, 1])
        send(j, 2, t.at[j, qb_up], r2in.at[j, 0], b_up)
        send(j, 2, t.at[j, qb_dn], r2in.at[j, 1], b_dn)
        send(j, 2, t.at[j, qb_op], r2in.at[j, 2], b_op)

    def r4(j):
        got(j, 2, r2in.at[j])
        total = (t[j, pb] + r2in[j, 2]) + (r2in[j, 0] + r2in[j, 1])
        w[j] = total / TOKENS + DAMP * d[j]

    def drain(low):
        for j in range(BLOCKS):
            if low and j == BLOCKS - 1:
                for h in range(2):
                    sent(j, 2 * h, d0b.at[j, pl.ds(2 * h, 2)])
            else:
                sent(j, 0, (d0b if low else d0).at[j])
            if low:
                sent(j, 1, din.at[j, pl.ds(1, 15)])
            else:
                sent(j, 1, rin.at[j])
                sent(j, 2, r2in.at[j])

    def transpose(k0, k1):
        @pl.loop(k0, k1)
        def _(k):
            r = pl.ds(pl.multiple_of(k * 256, 256), 256)
            ft[:, r] = f[r, :].T

    def operator_first():
        for j in range(BLOCKS):
            vb[j] = d[j].astype(BF)
        for i in range(2):
            xsrc[i] = g[i]
        pl.semaphore_wait(barrier, 7 + N_MP - 1)
        ag.first(0)
        ag.first(1)
        f_loads[0].wait()
        f_loads[1].wait()
        transpose(0, 6)
        ag.second(0)
        ag.first(2)
        ag.first(3)
        ag.second(1)
        xg.first(0)
        xg.first(1)
        f_loads[2].wait()
        f_loads[3].wait()
        transpose(6, 12)
        ag.third(0)
        ag.second(2)
        ag.second(3)
        c_load.wait()
        fill(0)

        @pl.loop(0, BLOCKS)
        def _(j):
            p1(j)

            @pl.when(j < BLOCKS - 1)
            def _():
                ag.third(j + 1)

            @pl.when(j >= 1)
            def _():
                r1(j - 1, False)

            @pl.when(j == 0)
            def _():
                xg.second(0)
                xg.second(1)

            @pl.when(j == 3)
            def _():
                r3(0)

            p2_start(j, False)

            @pl.when(j == 3)
            def _():
                r3(1)

            @pl.when(j < BLOCKS - 1)
            def _():
                fill(j + 1)

            @pl.when((j >= 1) & (j < 3))
            def _():
                xg.third(j - 1)

            p2_end(j, False)

        last = BLOCKS - 1
        r1(last, False)
        r4(last - 3)
        xsrc[2] = w[0]
        xg.first(2)
        r3(last - 1)
        r4(last - 2)
        xsrc[3] = w[1]
        xg.first(3)
        r3(last)
        xg.second(2)
        r4(last - 1)
        r4(last)

    def operator_second(step, beta):
        for j in (2, 3):
            near = d[j].astype(BF)
            vb[j] = near
            lsrc[j - 2] = (d[j] - near.astype(F32)).astype(BF)
        ag.first(2)
        ag.first(3)
        lg.first(0)
        lg.first(1)
        local(0, step, beta)

        @pl.loop(0, BLOCKS)
        def _(j):
            p1(j)

            @pl.when(j == 0)
            def _():
                xg.third(3)

            @pl.when(j == 1)
            def _():
                pd(0)

            @pl.when(j == 2)
            def _():
                pd(1)

            @pl.when(j == 3)
            def _():
                lg.third(1)
                lg.landed(0)
                pd_rest(2)

            @pl.when(j >= 1)
            def _():
                r1(j - 1, True)

            p2_start(j, True)

            @pl.when(j == 0)
            def _():
                xg.drain(1)
                xg.landed(1)
                xg.landed(3)
                ag.second(2)
                ag.second(3)
                local(1, step, beta)

            @pl.when(j == 1)
            def _():
                ag.third(2)
                ag.third(3)

            @pl.when(j == 2)
            def _():
                lg.third(0)
                fill(3)

            @pl.when(j >= 3)
            def _():
                r4_low(j - 3)

            p2_end(j, True)

            @pl.when(j == 0)
            def _():
                lg.second(0)
                lg.second(1)

            @pl.when(j == 1)
            def _():
                fill(2)

        last = BLOCKS - 1
        r1_half(last, 0)
        lg.landed(1)
        pd_rest(3)
        dv = d[...]
        value = total(pdv[...]) / TOKENS + DAMP * total(dv * dv)
        one_row[...] = jnp.broadcast_to(value, (1, 128))

        to_far(one_row, one_tab, 1)
        to_near(one_row, one_tab, 1)
        r1_half(last, 1)
        r4_low(last - 2)

        r4_low(last - 1)
        r4_low(last)
        from_all(one_tab, 1)

    def total(x):
        return jnp.sum(jnp.sum(jnp.sum(x, axis=0), axis=0, keepdims=True), axis=1, keepdims=True)

    def to_device(src, dst, i, dp, mp):
        pltpu.make_async_remote_copy(
            src_ref=src, dst_ref=dst.at[mx * GROUP + me], send_sem=es.at[i], recv_sem=er.at[i],
            device_id={"dp": dp, "mp": mp}, device_id_type=MESH,
        ).start()

    def to_group(src, dst, i, k):
        mp = lax.rem(mx + k, N_MP)

        @pl.loop(0, GROUP, unroll=8)
        def _(q):
            to_device(src, dst, i, lax.rem(me + q + GROUP // 2 + 2, GROUP), mp)

    def to_far(src, dst, i):
        to_group(src, dst, i, 2)
        to_group(src, dst, i, 1)

    def to_near(src, dst, i):
        to_group(src, dst, i, 3)

        @pl.loop(1, GROUP)
        def _(q):
            to_device(src, dst, i, lax.rem(me + q, GROUP), mx)

        dst[mx * GROUP + me] = src[...]

    def from_all(dst, i):
        rest = dst.at[pl.ds(0, GROUP * N_MP - 1)]
        copy(rest, rest, es.at[i], er.at[i], partner).wait()

    lane = lax.broadcasted_iota(jnp.int32, (1, 128), 1)

    def at_lane(x, k):
        return jnp.sum(jnp.where(lane == k, x, 0.0), axis=1, keepdims=True)

    def scalars(tb):
        sums, x = tb[:, 0:1, :], tb[:, 1:2, :]
        all_sums = jnp.sum(sums, axis=0)
        norm = at_lane(all_sums, 3)
        step = norm / at_lane(all_sums, 4)
        gap = x - step[None]
        at = lane[None]
        factor = jnp.where(at == 0, 1.0, jnp.where(at == 1, gap, jnp.where(at == 2, gap * gap, 0.0)))
        return norm, step, jnp.sum(jnp.sum(sums * factor, axis=0), axis=1, keepdims=True)

    def ratio(p, q):
        return jnp.where(q > 0, p / jnp.where(q > 0, q, 1.0), 0.0)

    pltpu.make_async_copy(g, g, ld.at[0]).wait()
    d[...] = g[...]
    operator_first()
    gv, wv = g[...], w[...]
    gg, gw, ww = total(gv * gv), total(gv * wv), total(wv * wv)
    x = ratio(gw, ww)
    u = gv - x * wv
    for j in range(BLOCKS):
        ag.drain(j)
    packed = jnp.zeros((1, 128), F32)
    for k, value in enumerate((total(u * u), 2.0 * total(u * wv), ww, gg, gw)):
        packed = jnp.where(lane == k, value, packed)
    row[0:1, :] = packed
    row[1:2, :] = jnp.broadcast_to(x, (1, 128))
    to_far(row, tab, 0)
    to_near(row, tab, 0)
    xg.second(3)
    xg.third(2)
    drain(False)
    xg.drain(0)
    xg.landed(0)
    xg.landed(2)
    from_all(tab, 0)
    norm, step, norm_next = scalars(tab[...])
    beta = norm_next / norm
    sol[...] = step * gv
    res = gv - step * wv
    g[...] = res
    d[...] = res + beta * gv
    operator_second(step, beta)
    step = norm_next / jnp.sum(one_tab[...], axis=0)[:, :1]
    dv, wv = d[...], w[...]
    for j in range(BLOCKS):
        cols = pl.ds(j * NB, NB)
        sol_o[:, cols] = sol[j] + step * dv[j]
        res_o[:, cols] = g[j] - step * wv[j]
    drain(True)
    for j in (2, 3):
        ag.drain(j)
        xg.drain(j)
        lg.drain(j - 2)


def shards(features, curvature, task_grad):
    any_spec = pl.BlockSpec(memory_space=pltpu.HBM)
    out = jax.ShapeDtypeStruct(task_grad.shape, F32)
    small = (BLOCKS, ROWS, NB)
    return pl.pallas_call(
        kernel,
        out_shape=(out, out),
        in_specs=[any_spec] * 3,
        out_specs=(pl.BlockSpec(memory_space=pltpu.VMEM),) * 2,
        scratch_shapes=[
            pltpu.VMEM((TOK, DIN), BF),
            pltpu.VMEM((DIN, TOK), BF),
            pltpu.VMEM((TOK, COLS), BF),
            pltpu.VMEM(small, F32),
            pltpu.VMEM(small, F32),
            pltpu.VMEM(small, F32),
            pltpu.VMEM(small, F32),
            pltpu.VMEM(small, BF),
            pltpu.VMEM((BLOCKS, 16, ROWS, NB), BF),
            pltpu.VMEM((BLOCKS, 16, ROWS, NB), BF),
            pltpu.VMEM((BLOCKS, RING, RING, 2, ROWS, NB), BF),
            pltpu.VMEM((TOK, NB), BF),
            pltpu.VMEM((BLOCKS, RING, RING, 2, ROWS, NB), F32),
            pltpu.VMEM((BLOCKS, RING, RING, 2, ROWS, NB), BF),
            pltpu.VMEM((BLOCKS, RING, RING, ROWS, NB), F32),
            pltpu.VMEM((BLOCKS, RING, RING, ROWS, NB), BF),
            pltpu.VMEM((BLOCKS, 16, ROWS, NB), F32),
            pltpu.VMEM((BLOCKS, 16, ROWS, NB), BF),
            pltpu.VMEM((BLOCKS, 3, RING, ROWS, NB), F32),
            pltpu.VMEM((BLOCKS, RING, ROWS, NB), F32),
            pltpu.VMEM((BLOCKS, 3, ROWS, NB), F32),
            pltpu.VMEM((BLOCKS, 16, ROWS, NB), BF),
            pltpu.VMEM((4, ROWS, NB), F32),
            pltpu.VMEM((4, 16, ROWS, NB), F32),
            pltpu.VMEM((4, 16, ROWS, NB), F32),
            pltpu.VMEM((2, ROWS, NB), BF),
            pltpu.VMEM((2, 16, ROWS, NB), BF),
            pltpu.VMEM((2, 16, ROWS, NB), BF),
            pltpu.VMEM(small, F32),
            pltpu.VMEM((2, 128), F32),
            pltpu.VMEM((GROUP * N_MP, 2, 128), F32),
            pltpu.VMEM((1, 128), F32),
            pltpu.VMEM((GROUP * N_MP, 1, 128), F32),
            pltpu.SemaphoreType.DMA((BLOCKS + 4, 3)),
            pltpu.SemaphoreType.DMA((BLOCKS + 4, 3)),
            pltpu.SemaphoreType.DMA((BLOCKS, 3)),
            pltpu.SemaphoreType.DMA((BLOCKS, 3)),
            pltpu.SemaphoreType.DMA((2,)),
            pltpu.SemaphoreType.DMA((2,)),
            pltpu.SemaphoreType.DMA((6,)),
        ],
        compiler_params=pltpu.CompilerParams(
            collective_id=0, has_side_effects=True, vmem_limit_bytes=51 * 2**20
        ),
    )(features, curvature, pltpu.with_memory_space_constraint(task_grad, pltpu.HBM))


def solution(mesh):
    placed = (P("dp", None), P("dp", "mp"), P("dp", "mp"))
    return jax.shard_map(
        shards,
        mesh=mesh,
        in_specs=placed,
        out_specs=(P("dp", "mp"), P("dp", "mp")),
        check_vma=False,
    )
```

```python
import functools

import jax
import jax.numpy as jnp
from jax import lax
from jax.experimental import pallas as pl
from jax.experimental.pallas import tpu as pltpu
from jax.sharding import PartitionSpec as P

RING = 4
GROUP = 32
N_MP = 4
TOK = 3072
DIN = 1024
COLS = 1024
NB = 256
BLOCKS = COLS // NB
ROWS = DIN // GROUP
TOKENS = 98304.0
DAMP = 0.5
MESH = pl.DeviceIdType.MESH
BF, F32 = jnp.bfloat16, jnp.float32
FAR_FIRST = sorted(
    ((i, k) for i in range(RING) for k in range(RING) if i or k),
    key=lambda t: -min(t[0], RING - t[0]) - min(t[1], RING - t[1]),
)


def kernel(
    f_h, c_h, g_h, sol_o, res_o,
    f, ft, cv, g, d, w, sol, vb, g_own, g_par, v, wt,
    acc, accb, d0, d0b, s, sb, rin, t, r2in,
    din, xsrc, xo, xp, lsrc, lo, lp, pdv, row, tab, one_row, one_tab,
    gs, gr, qs, qr, es, er, ld,
):
    me = lax.axis_index("dp")
    mx = lax.axis_index("mp")
    c = lax.rem(me, 2)
    chip = me // 2
    z = chip // RING
    y = lax.rem(chip, RING)
    pa = (1 - c) * y + c * z
    pb = (1 - c) * z + c * y

    def a_at(k):
        q = lax.rem(pa + k, RING)
        return ((1 - c) * (z * RING + q) + c * (q * RING + y)) * 2 + c

    def b_at(k):
        q = lax.rem(pb + k, RING)
        return ((1 - c) * (q * RING + y) + c * (z * RING + q)) * 2 + c

    partner = me + 1 - 2 * c
    a_up, a_dn, a_op = a_at(1), a_at(3), a_at(2)
    b_up, b_dn, b_op = b_at(1), b_at(3), b_at(2)
    qa_up, qa_dn, qa_op = lax.rem(pa + 1, RING), lax.rem(pa + 3, RING), lax.rem(pa + 2, RING)
    qb_up, qb_dn, qb_op = lax.rem(pb + 1, RING), lax.rem(pb + 3, RING), lax.rem(pb + 2, RING)

    loads = [
        pltpu.make_async_copy(g_h.at[:, pl.ds(j * NB, NB)], g.at[j], ld.at[0])
        for j in range(BLOCKS)
    ]
    parts = 4
    f_loads = [
        pltpu.make_async_copy(
            f_h.at[pl.ds(k * (TOK // parts), TOK // parts)],
            f.at[pl.ds(k * (TOK // parts), TOK // parts)],
            ld.at[1 + k],
        )
        for k in range(parts)
    ]
    c_load = pltpu.make_async_copy(c_h, cv, ld.at[1 + parts])
    for x in (*loads, *f_loads, c_load):
        x.start()

    barrier = pltpu.get_barrier_semaphore()

    for q in (a_up, a_dn, a_op, b_up, b_dn, b_op, partner):
        pl.semaphore_signal(barrier, inc=1, device_id={"dp": q}, device_id_type=MESH)

    for k in range(1, N_MP):
        pl.semaphore_signal(
            barrier, inc=1, device_id={"mp": lax.rem(mx + k, N_MP)}, device_id_type=MESH
        )

    def copy(src, dst, sends, recvs, dev):
        return pltpu.make_async_remote_copy(
            src_ref=src, dst_ref=dst, send_sem=sends, recv_sem=recvs,
            device_id={"dp": dev}, device_id_type=MESH,
        )

    def send(j, i, src, dst, dev):
        copy(src, dst, qs.at[j, i], qr.at[j, i], dev).start()

    def got(j, i, whole):
        copy(whole, whole, qs.at[j, i], qr.at[j, i], partner).wait_recv()

    def sent(j, i, whole):
        copy(whole, whole, qs.at[j, i], qr.at[j, i], partner).wait_send()

    def strip(buf, j, q):
        return buf.at[j, pl.ds(q * RING, RING)]

    class Gather:
        def __init__(self, src, own, par, base):
            self.src, self.own, self.par, self.base = src, own, par, base

        def copy(self, j, i, src, dst, dev):
            return copy(src, dst, gs.at[self.base + j, i], gr.at[self.base + j, i], dev)

        def got(self, j, i, pieces):
            part = self.own.at[j, pl.ds(0, pieces)]
            self.copy(j, i, part, part, partner).wait_recv()

        def first(self, j):
            at = pb * RING + pa
            for dev in (a_up, a_dn, a_op):
                self.copy(j, 0, self.src.at[j], self.own.at[j, at], dev).start()
            self.own[j, at] = self.src[j]

        def second(self, j):
            self.got(j, 0, 3)
            mine = strip(self.own, j, pb)
            for dev in (b_up, b_dn, b_op):
                self.copy(j, 1, mine, mine, dev).start()
            self.copy(j, 2, mine, strip(self.par, j, pb), partner).start()

        def third(self, j):
            self.got(j, 1, 12)
            for q in (qb_dn, qb_up, qb_op):
                self.copy(j, 2, strip(self.own, j, q), strip(self.par, j, q), partner).start()

        def landed(self, j):
            self.got(j, 2, 16)

        def drain(self, j):
            for i, pieces in enumerate((3, 12, 16)):
                part = self.own.at[j, pl.ds(0, pieces)]
                self.copy(j, i, part, part, partner).wait_send()

    ag = Gather(vb, g_own, g_par, 0)
    xg = Gather(xsrc, xo, xp, BLOCKS)
    lg = Gather(lsrc, lo, lp, 0)

    def places():
        for zz in range(RING):
            for yy in range(RING):
                zy, yz = zz * RING + yy, yy * RING + zz
                yield zz, yy, (1 - c) * zy + c * yz, (1 - c) * yz + c * zy

    def fill(j):
        ag.landed(j)
        for zz, yy, mine, other in places():
            v[j, zz, yy, c] = g_own[j, mine]
            v[j, zz, yy, 1 - c] = g_par[j, other]

    def local(j, step, beta):
        for zz, yy, mine, other in places():
            for buf, at, core in ((xo, mine, c), (xp, other, 1 - c)):
                gv = buf[j, at]
                nxt = (gv - step * buf[2 + j, at]) + beta * gv
                buf[j, at] = nxt
                v[j, zz, yy, core] = nxt.astype(BF)

    def pd(j):
        part = jnp.zeros((ROWS, NB), F32)
        for zz, yy, mine, other in places():
            part += acc[j, zz, yy, c] * xo[j, mine] + acc[j, zz, yy, 1 - c] * xp[j, other]
        pdv[j] = part

    def pd_rest(j):
        part = jnp.zeros((ROWS, NB), F32)
        for zz, yy, mine, other in places():
            for core, rest in ((c, lo[j - 2, mine]), (1 - c, lp[j - 2, other])):
                part += acc[j, zz, yy, core] * (v[j, zz, yy, core].astype(F32) + rest.astype(F32))
        pdv[j] = part

    def alone(j):
        return pl.loop(0, (j + BLOCKS) // BLOCKS)

    def p1(j):
        cols = pl.ds(pl.multiple_of(j * NB, NB), NB)

        @alone(j)
        def _(_):
            p = jnp.dot(f[...], v[j].reshape(DIN, NB), preferred_element_type=F32)
            wt[...] = (cv[:, cols].astype(F32) * p).astype(BF)

    def p2(j, z0, zn, low, i=0):
        r = pl.ds(z0 * (DIN // RING), zn * (DIN // RING))
        zs = pl.ds(z0, zn)

        @alone(j)
        def _(_):
            out = jnp.dot(ft[r, :], wt[...], preferred_element_type=F32)
            out = out.reshape(zn, RING, 2, ROWS, NB)
            acc[j, zs] = out
            if low:
                accb[j, zs] = out.astype(BF)

        src, dst = (accb, d0b) if low else (acc, d0)
        send(j, i, src.at[j, zs, :, 1 - c], dst.at[j, zs], partner)

    def p2_start(j, low):
        halves = j % 2 == 1 if low else j == BLOCKS - 1

        @pl.when(~halves)
        def _():
            p2(j, 0, RING, low)

        @pl.when(halves)
        def _():
            p2(j, 0, RING // 2, low)

    def p2_end(j, low):
        @pl.when(j % 2 == 1 if low else j == BLOCKS - 1)
        def _():
            p2(j, RING // 2, RING // 2, low, 3 * (j // (BLOCKS - 1)))

    def r1(j, low):
        src = d0b if low else d0
        got(j, 0, src.at[j])
        for zz, yy, _, at in places():
            both = acc[j, zz, yy, c] + src[j, zz, yy].astype(F32)
            s[j, at] = both
            if low:
                sb[j, at] = both.astype(BF)
        if low:
            for ka, kb in FAR_FIRST:
                piece(j, ka, kb)
        else:
            send(j, 1, strip(s, j, qa_up), rin.at[j, 0], a_up)
            send(j, 1, strip(s, j, qa_dn), rin.at[j, 1], a_dn)
            send(j, 1, strip(s, j, qa_op), rin.at[j, 2], a_op)

    def r1_part(j, h):
        got(j, 3 * h, d0.at[j, pl.ds(2 * h, 2)])
        for zz, yy, _, at in places():
            if zz // 2 == h:
                s[j, at] = acc[j, zz, yy, c] + d0[j, zz, yy]

        @pl.when(c == 0)
        def _():
            for i, (q, dev) in enumerate(((qa_up, a_up), (qa_dn, a_dn), (qa_op, a_op))):
                part = s.at[j, pl.ds(q * RING + 2 * h, 2)]
                send(j, 1, part, rin.at[j, i, pl.ds(2 * h, 2)], dev)

        @pl.when(c == 1)
        def _():
            for q in (2 * h, 2 * h + 1):

                @pl.when(pa != q)
                def _(q=q):
                    ka = lax.rem(q + RING - pa, RING)
                    slot = lax.rem(2 * (ka + 2), 3)
                    send(j, 1, s.at[j, pl.ds(q * RING, RING)], rin.at[j, slot], (q * RING + y) * 2 + c)

    def r1_half(j, h):
        got(j, 3 * h, d0b.at[j, pl.ds(2 * h, 2)])
        for zz, yy, _, at in places():
            if zz // 2 == h:
                both = acc[j, zz, yy, c] + d0b[j, zz, yy].astype(F32)
                s[j, at] = both
                sb[j, at] = both.astype(BF)
        for zz, yy, _, at in places():
            if zz // 2 == h:

                @pl.when((zz != z) | (yy != y))
                def _(zz=zz, yy=yy, at=at):
                    ka = lax.rem((1 - c) * yy + c * zz + RING - pa, RING)
                    kb = lax.rem((1 - c) * zz + c * yy + RING - pb, RING)
                    send(j, 1, sb.at[j, at], din.at[j, ka * RING + kb], (zz * RING + yy) * 2 + c)

    def piece(j, ka, kb):
        qa, qb = lax.rem(pa + ka, RING), lax.rem(pb + kb, RING)
        dev = ((1 - c) * (qb * RING + qa) + c * (qa * RING + qb)) * 2 + c
        send(j, 1, sb.at[j, qa * RING + qb], din.at[j, ka * RING + kb], dev)

    def r4_low(j):
        got(j, 1, din.at[j, pl.ds(1, 15)])
        total = s[j, pa * RING + pb]
        for k in range(1, 16):
            total += din[j, k].astype(F32)
        w[j] = total / TOKENS + DAMP * d[j]

    def r3(j):
        got(j, 1, rin.at[j])
        mine = s[j, pl.ds(pa * RING, RING)]
        t[j] = (mine + rin[j, 2]) + (rin[j, 0] + rin[j, 1])
        send(j, 2, t.at[j, qb_up], r2in.at[j, 0], b_up)
        send(j, 2, t.at[j, qb_dn], r2in.at[j, 1], b_dn)
        send(j, 2, t.at[j, qb_op], r2in.at[j, 2], b_op)

    def r4(j):
        got(j, 2, r2in.at[j])
        total = (t[j, pb] + r2in[j, 2]) + (r2in[j, 0] + r2in[j, 1])
        w[j] = total / TOKENS + DAMP * d[j]

    def drain(low):
        for j in range(BLOCKS):
            src = d0b if low else d0
            if j == BLOCKS - 1:
                for h in range(2):
                    sent(j, 3 * h, src.at[j, pl.ds(2 * h, 2)])
            else:
                sent(j, 0, src.at[j])
            if low:
                sent(j, 1, din.at[j, pl.ds(1, 15)])
            else:
                sent(j, 1, rin.at[j])
                sent(j, 2, r2in.at[j])

    def transpose(k0, k1):
        @pl.loop(k0, k1)
        def _(k):
            r = pl.ds(pl.multiple_of(k * 256, 256), 256)
            ft[:, r] = f[r, :].T

    def operator_first():
        for j in range(BLOCKS):
            vb[j] = d[j].astype(BF)
        for i in range(2):
            xsrc[i] = g[i]
        pl.semaphore_wait(barrier, 7 + N_MP - 1)
        ag.first(0)
        ag.first(1)
        f_loads[0].wait()
        f_loads[1].wait()
        transpose(0, 6)
        ag.second(0)
        ag.first(2)
        ag.first(3)
        ag.second(1)
        xg.first(0)
        xg.first(1)
        f_loads[2].wait()
        f_loads[3].wait()
        transpose(6, 12)
        ag.third(0)
        ag.second(2)
        ag.second(3)
        c_load.wait()
        fill(0)

        @pl.loop(0, BLOCKS)
        def _(j):
            p1(j)

            @pl.when(j < BLOCKS - 1)
            def _():
                ag.third(j + 1)

            @pl.when(j >= 1)
            def _():
                r1(j - 1, False)

            @pl.when(j == 0)
            def _():
                xg.second(0)
                xg.second(1)

            @pl.when(j == 3)
            def _():
                r3(0)

            p2_start(j, False)

            @pl.when(j == 3)
            def _():
                r3(1)

            @pl.when(j < BLOCKS - 1)
            def _():
                fill(j + 1)

            @pl.when((j >= 1) & (j < 3))
            def _():
                xg.third(j - 1)

            p2_end(j, False)

        last = BLOCKS - 1
        r1_part(last, 0)
        r1_part(last, 1)
        r4(last - 3)
        xsrc[2] = w[0]
        xg.first(2)
        r3(last - 1)
        r4(last - 2)
        xsrc[3] = w[1]
        xg.first(3)
        r3(last)
        xg.second(2)
        r4(last - 1)
        r4(last)

    def operator_second(step, beta):
        for j in (2, 3):
            near = d[j].astype(BF)
            vb[j] = near
            lsrc[j - 2] = (d[j] - near.astype(F32)).astype(BF)
        ag.first(2)
        ag.first(3)
        lg.first(0)
        lg.first(1)
        local(0, step, beta)

        @pl.loop(0, BLOCKS)
        def _(j):
            p1(j)

            @pl.when(j == 0)
            def _():
                xg.third(3)

            @pl.when(j == 1)
            def _():
                pd(0)

            @pl.when(j == 2)
            def _():
                pd(1)

            @pl.when(j == 3)
            def _():
                lg.third(1)
                lg.landed(0)
                pd_rest(2)

            @pl.when(j >= 1)
            def _():
                r1(j - 1, True)

            p2_start(j, True)

            @pl.when(j == 0)
            def _():
                xg.drain(1)
                xg.landed(1)
                xg.landed(3)
                ag.second(2)
                ag.second(3)
                local(1, step, beta)

            @pl.when(j == 1)
            def _():
                ag.third(2)
                ag.third(3)

            @pl.when(j == 2)
            def _():
                lg.third(0)
                fill(3)

            @pl.when(j >= 3)
            def _():
                r4_low(j - 3)

            p2_end(j, True)

            @pl.when(j == 0)
            def _():
                lg.second(0)
                lg.second(1)

            @pl.when(j == 1)
            def _():
                fill(2)

        last = BLOCKS - 1
        r1_half(last, 0)
        lg.landed(1)
        pd_rest(3)
        dv = d[...]
        value = total(pdv[...]) / TOKENS + DAMP * total(dv * dv)
        one_row[...] = jnp.broadcast_to(value, (1, 128))

        to_far(one_row, one_tab, 1)
        to_near(one_row, one_tab, 1)
        r1_half(last, 1)
        r4_low(last - 2)

        r4_low(last - 1)
        r4_low(last)
        from_all(one_tab, 1)

    def total(x):
        return jnp.sum(jnp.sum(jnp.sum(x, axis=0), axis=0, keepdims=True), axis=1, keepdims=True)

    def to_device(src, dst, i, dp, mp):
        pltpu.make_async_remote_copy(
            src_ref=src, dst_ref=dst.at[mx * GROUP + me], send_sem=es.at[i], recv_sem=er.at[i],
            device_id={"dp": dp, "mp": mp}, device_id_type=MESH,
        ).start()

    def to_group(src, dst, i, k):
        mp = lax.rem(mx + k, N_MP)

        @pl.loop(0, GROUP, unroll=8)
        def _(q):
            to_device(src, dst, i, lax.rem(me + q + GROUP // 2 + 2, GROUP), mp)

    def to_far(src, dst, i):
        to_group(src, dst, i, 2)
        to_group(src, dst, i, 1)

    def to_near(src, dst, i):
        to_group(src, dst, i, 3)

        @pl.loop(1, GROUP)
        def _(q):
            to_device(src, dst, i, lax.rem(me + q, GROUP), mx)

        dst[mx * GROUP + me] = src[...]

    def from_all(dst, i):
        rest = dst.at[pl.ds(0, GROUP * N_MP - 1)]
        copy(rest, rest, es.at[i], er.at[i], partner).wait()

    lane = lax.broadcasted_iota(jnp.int32, (1, 128), 1)

    def at_lane(x, k):
        return jnp.sum(jnp.where(lane == k, x, 0.0), axis=1, keepdims=True)

    def scalars(tb):
        sums, x = tb[:, 0:1, :], tb[:, 1:2, :]
        all_sums = jnp.sum(sums, axis=0)
        norm = at_lane(all_sums, 3)
        step = norm / at_lane(all_sums, 4)
        gap = x - step[None]
        at = lane[None]
        factor = jnp.where(at == 0, 1.0, jnp.where(at == 1, gap, jnp.where(at == 2, gap * gap, 0.0)))
        return norm, step, jnp.sum(jnp.sum(sums * factor, axis=0), axis=1, keepdims=True)

    def ratio(p, q):
        return jnp.where(q > 0, p / jnp.where(q > 0, q, 1.0), 0.0)

    pltpu.make_async_copy(g, g, ld.at[0]).wait()
    d[...] = g[...]
    operator_first()
    gv, wv = g[...], w[...]
    gg, gw, ww = total(gv * gv), total(gv * wv), total(wv * wv)
    x = ratio(gw, ww)
    u = gv - x * wv
    for j in range(BLOCKS):
        ag.drain(j)
    packed = jnp.zeros((1, 128), F32)
    for k, value in enumerate((total(u * u), 2.0 * total(u * wv), ww, gg, gw)):
        packed = jnp.where(lane == k, value, packed)
    row[0:1, :] = packed
    row[1:2, :] = jnp.broadcast_to(x, (1, 128))
    to_far(row, tab, 0)
    to_near(row, tab, 0)
    xg.second(3)
    xg.third(2)
    drain(False)
    xg.drain(0)
    xg.landed(0)
    xg.landed(2)
    from_all(tab, 0)
    norm, step, norm_next = scalars(tab[...])
    beta = norm_next / norm
    sol[...] = step * gv
    res = gv - step * wv
    g[...] = res
    d[...] = res + beta * gv
    operator_second(step, beta)
    step = norm_next / jnp.sum(one_tab[...], axis=0)[:, :1]
    dv, wv = d[...], w[...]
    for j in range(BLOCKS):
        cols = pl.ds(j * NB, NB)
        sol_o[:, cols] = sol[j] + step * dv[j]
        res_o[:, cols] = g[j] - step * wv[j]
    drain(True)
    for j in (2, 3):
        ag.drain(j)
        xg.drain(j)
        lg.drain(j - 2)


def shards(features, curvature, task_grad):
    any_spec = pl.BlockSpec(memory_space=pltpu.HBM)
    out = jax.ShapeDtypeStruct(task_grad.shape, F32)
    small = (BLOCKS, ROWS, NB)
    return pl.pallas_call(
        kernel,
        out_shape=(out, out),
        in_specs=[any_spec] * 3,
        out_specs=(pl.BlockSpec(memory_space=pltpu.VMEM),) * 2,
        scratch_shapes=[
            pltpu.VMEM((TOK, DIN), BF),
            pltpu.VMEM((DIN, TOK), BF),
            pltpu.VMEM((TOK, COLS), BF),
            pltpu.VMEM(small, F32),
            pltpu.VMEM(small, F32),
            pltpu.VMEM(small, F32),
            pltpu.VMEM(small, F32),
            pltpu.VMEM(small, BF),
            pltpu.VMEM((BLOCKS, 16, ROWS, NB), BF),
            pltpu.VMEM((BLOCKS, 16, ROWS, NB), BF),
            pltpu.VMEM((BLOCKS, RING, RING, 2, ROWS, NB), BF),
            pltpu.VMEM((TOK, NB), BF),
            pltpu.VMEM((BLOCKS, RING, RING, 2, ROWS, NB), F32),
            pltpu.VMEM((BLOCKS, RING, RING, 2, ROWS, NB), BF),
            pltpu.VMEM((BLOCKS, RING, RING, ROWS, NB), F32),
            pltpu.VMEM((BLOCKS, RING, RING, ROWS, NB), BF),
            pltpu.VMEM((BLOCKS, 16, ROWS, NB), F32),
            pltpu.VMEM((BLOCKS, 16, ROWS, NB), BF),
            pltpu.VMEM((BLOCKS, 3, RING, ROWS, NB), F32),
            pltpu.VMEM((BLOCKS, RING, ROWS, NB), F32),
            pltpu.VMEM((BLOCKS, 3, ROWS, NB), F32),
            pltpu.VMEM((BLOCKS, 16, ROWS, NB), BF),
            pltpu.VMEM((4, ROWS, NB), F32),
            pltpu.VMEM((4, 16, ROWS, NB), F32),
            pltpu.VMEM((4, 16, ROWS, NB), F32),
            pltpu.VMEM((2, ROWS, NB), BF),
            pltpu.VMEM((2, 16, ROWS, NB), BF),
            pltpu.VMEM((2, 16, ROWS, NB), BF),
            pltpu.VMEM(small, F32),
            pltpu.VMEM((2, 128), F32),
            pltpu.VMEM((GROUP * N_MP, 2, 128), F32),
            pltpu.VMEM((1, 128), F32),
            pltpu.VMEM((GROUP * N_MP, 1, 128), F32),
            pltpu.SemaphoreType.DMA((BLOCKS + 4, 3)),
            pltpu.SemaphoreType.DMA((BLOCKS + 4, 3)),
            pltpu.SemaphoreType.DMA((BLOCKS, 4)),
            pltpu.SemaphoreType.DMA((BLOCKS, 4)),
            pltpu.SemaphoreType.DMA((2,)),
            pltpu.SemaphoreType.DMA((2,)),
            pltpu.SemaphoreType.DMA((6,)),
        ],
        compiler_params=pltpu.CompilerParams(
            collective_id=0, has_side_effects=True, vmem_limit_bytes=51 * 2**20
        ),
    )(features, curvature, pltpu.with_memory_space_constraint(task_grad, pltpu.HBM))


def solution(mesh):
    placed = (P("dp", None), P("dp", "mp"), P("dp", "mp"))
    return jax.shard_map(
        shards,
        mesh=mesh,
        in_specs=placed,
        out_specs=(P("dp", "mp"), P("dp", "mp")),
        check_vma=False,
    )
```
